256 devices in a mesh: ang: 8 (over x_hi, y), strip: 32 (over x_lo, z, core).
Axes of the slice: x: 4 (x_hi: 2, x_lo: 2; x = x_hi * 2 + x_lo), y: 4, z: 8, core: 2. Of those that a mesh axis runs over, the one named last changes fastest.
Arguments:
- slab: bfloat16 [8, 2, 4096, 512], P('ang', None, 'strip'), may hold values from -6 to 6
- shear_taps: float32 [4, 8, 8], replicated, may hold values from -1 to 1
- band_offsets: int32 [8, 8], replicated, may hold values from -64 to 64
- probe: bfloat16 [2, 256, 256], replicated, may hold values from -6 to 6
- scan_rows: int32 [8, 128], P('ang', 'strip'), may hold values from 0 to 127
- scan_columns: int32 [8, 128], P('ang', 'strip'), may hold values from 0 to 256
- frame_counts: int32 [8, 32], P('ang', 'strip'), may hold values from 1 to 4, 64 in all within a row
- amplitudes: bfloat16 [8, 128, 256, 256], P('ang', 'strip'), may hold values from 0.19921875 to 4
Outputs:
- slab_grad: float32 [8, 2, 4096, 512], P('ang', None, 'strip')
The draws below stay inside these ranges and needn't reach their ends.
Inputs may be any that keep to these rules, and one draw needn't show every extreme that they name: `frame_counts`: for every angle the counts over the 32 strips sum to 64, and some strip has exactly 4 frames.
All inputs are finite; a program needn't handle non-finite values. No bound on the sum of `frame_counts` on one device may be relied on, other than what follows from the above.
Results may differ from the reference program's by a relative error of at most 0.013.
Values may be sent and summed in bfloat16 or wider, within the bound.
No kernel may reach another device: no remote copies, remote signals or barrier semaphores. Data moves between devices by JAX's collectives and lax.ppermute only.
A program may use at most 64 MiB of HBM per device.

```python
import math
import jax
import jax.numpy as jnp
import numpy as np
from jax import lax

ROWS_DEV = 128
COLS = 512
FRAME = 256
TAPS = 4
MAXSHIFT = 64
MEAN = 2
CAP = 4
ANGLES = 8
SLICES = 8
STRIPS = 32
NROWS = 4096


def plant(values, key, smallest, largest):
    spot = [jax.random.randint(jax.random.fold_in(key, axis), (), 0, length) for axis, length in enumerate(values.shape)]
    main_axis = values.shape.index(max(values.shape))
    neighbour = spot[:main_axis] + [(spot[main_axis] + 1) % values.shape[main_axis]] + spot[main_axis + 1:]
    return values.at[tuple(spot)].set(smallest).at[tuple(neighbour)].set(largest)


def level_of(rng, dims, pieces, least, top_value):
    def one(axis_at, parts):
        draws = jax.random.uniform(jax.random.fold_in(jax.random.fold_in(rng, 6), axis_at), (parts,), jnp.float32, least / len(pieces), top_value / len(pieces))
        return jnp.repeat(jnp.exp(draws), dims[axis_at] // parts).reshape((-1,) + (1,) * (len(dims) - axis_at - 1))

    factor_of = one(*pieces[0])
    for cut in pieces[1:]:
        factor_of = factor_of * one(*cut)
    return factor_of


def split_up(amount, total, reach, lean):
    loads = [(1 << 20) // math.isqrt(rank ** lean) + 1 for rank in range(2, amount + 1)]
    spare, holding = total - reach - (amount - 1), [1] * (amount - 1)
    while spare > 0:
        movable = [i for i in range(amount - 1) if holding[i] < reach]
        whole, left = sum([loads[i] for i in movable]), spare
        for i in movable:
            more = min(reach - holding[i], max(1, left * loads[i] // whole), spare)
            holding[i] = holding[i] + more
            spare = spare - more
    return np.array([reach] + holding)


def ragged(key, number_of, total, limit, skew):
    if number_of == 2:
        one = jax.random.randint(key, (), max(1, total - limit), min(limit, total - 1) + 1)
        return jnp.stack([one, total - one])
    sizes = jnp.asarray(split_up(number_of, total, limit, skew), jnp.int32)
    twos = (number_of - 1) // 2
    giver, receiver = sizes[1:1 + 2 * twos:2], sizes[2:2 + 2 * twos:2]
    slack = jnp.minimum(giver - 1, limit - receiver)
    moved = jax.random.randint(jax.random.fold_in(key, 1), (twos,), 0, 1 << 20) % (slack + 1)
    sizes = sizes.at[1:1 + 2 * twos:2].set(giver - moved).at[2:2 + 2 * twos:2].set(receiver + moved)
    return sizes[jax.random.permutation(jax.random.fold_in(key, 2), number_of)]


def centred(key, extent, scale, reach, split=(), held_as=jnp.bfloat16):
    level = level_of(key, extent, split, -0.22, 0.18) if split else 1.0
    result = jax.random.normal(key, extent, jnp.float32) * scale * level
    return jnp.minimum(jnp.maximum(result, -reach), reach).astype(held_as)


def setup_inputs(seed: int = 0) -> dict:
    keys = jax.random.split(jax.random.key(seed), 9)
    return {
        "slab": centred(keys[0], (SLICES, 2, NROWS, COLS), 1.0, 6.0, ((0, 8), (2, 32))),
        "shear_taps": centred(keys[1], (TAPS, ANGLES, SLICES), (SLICES * TAPS) ** -0.5, 1.0, (), jnp.float32),
        "band_offsets": plant(jax.random.randint(keys[2], (ANGLES, SLICES), 0 - MAXSHIFT, MAXSHIFT + 1), jax.random.fold_in(keys[2], 1), 0 - MAXSHIFT, MAXSHIFT).astype(jnp.int32),
        "probe": centred(keys[3], (2, FRAME, FRAME), 1.0, 6.0),
        "scan_rows": plant(jax.random.randint(keys[4], (ANGLES, STRIPS * CAP), 0, ROWS_DEV), jax.random.fold_in(keys[4], 1), 0, ROWS_DEV - 1).astype(jnp.int32),
        "scan_columns": plant(jax.random.randint(keys[5], (ANGLES, STRIPS * CAP), 0, COLS - FRAME + 1), jax.random.fold_in(keys[5], 1), 0, COLS - FRAME).astype(jnp.int32),
        "frame_counts": jax.vmap(lambda own: ragged(own, STRIPS, MEAN * STRIPS, CAP, 2))(jax.random.split(keys[6], ANGLES)).reshape((ANGLES, STRIPS)).astype(jnp.int32),
        "amplitudes": jnp.clip(jnp.exp(math.log(4.0) - 2.9996462 * jax.random.uniform(keys[7], (ANGLES, STRIPS * CAP, FRAME, FRAME), jnp.float32) ** level_of(keys[7], (ANGLES, STRIPS * CAP, FRAME, FRAME), ((0, 8), (1, 32)), -0.2, 0.2)), 0.19921875, 4.0).astype(jnp.bfloat16),
    }


def dft_tables(length):
    index = jnp.arange(length, dtype=jnp.int32)
    product = index[:, None] * index[None, :] % length
    phase = product.astype(jnp.float32) * (2.0 * math.pi / length)
    scale = 1.0 / math.sqrt(length)
    return ((jnp.cos(phase) * scale).astype(jnp.bfloat16), (jnp.sin(phase) * scale).astype(jnp.bfloat16))

def product_left(matrix, batch):
    return jnp.einsum('ij,bjk->bik', matrix.astype(jnp.float32), batch.astype(jnp.float32), precision=lax.Precision.HIGHEST)

def product_right(batch, matrix):
    return jnp.einsum('bij,jk->bik', batch.astype(jnp.float32), matrix.astype(jnp.float32), precision=lax.Precision.HIGHEST)

def frame_gradient(patch, probe, amplitudes):
    length = probe.shape[1]
    cosine, sine = dft_tables(length)
    forward_left = jnp.concatenate([jnp.concatenate([cosine, sine], 1), jnp.concatenate([-sine, cosine], 1)], 0)
    inverse_left = jnp.concatenate([jnp.concatenate([cosine, -sine], 1), jnp.concatenate([sine, cosine], 1)], 0)
    right = jnp.concatenate([cosine, sine], 1)
    probe_real = probe[0].astype(jnp.float32)
    probe_imag = probe[1].astype(jnp.float32)
    patch_real = patch[:, 0]
    patch_imag = patch[:, 1]
    exit_wave = jnp.concatenate([probe_real * patch_real - probe_imag * patch_imag, probe_real * patch_imag + probe_imag * patch_real], axis=1).astype(jnp.bfloat16)
    half = product_left(forward_left, exit_wave).astype(jnp.bfloat16)
    far = product_right(half, right)
    far_real = far[:, :length, :length] + far[:, length:, length:]
    far_imag = far[:, length:, :length] - far[:, :length, length:]
    factor = 1.0 - amplitudes.astype(jnp.float32) / jnp.sqrt(far_real * far_real + far_imag * far_imag + 1.0)
    residual = jnp.concatenate([far_real * factor, far_imag * factor], axis=1).astype(jnp.bfloat16)
    back_half = product_left(inverse_left, residual).astype(jnp.bfloat16)
    back = product_right(back_half, right)
    back_real = back[:, :length, :length] - back[:, length:, length:]
    back_imag = back[:, length:, :length] + back[:, :length, length:]
    grad_real = probe_real * back_real + probe_imag * back_imag
    grad_imag = probe_real * back_imag - probe_imag * back_real
    return jnp.stack([grad_real, grad_imag], axis=1)

def add_taps(total, source, shear_taps, band_offsets, angle, depth, sign, width):
    margin = MAXSHIFT + TAPS
    for tap in range(TAPS):
        start = (margin + sign * (band_offsets[angle, depth] + tap)).astype(jnp.int32)
        piece = lax.dynamic_slice_in_dim(source, start, width, axis=2)
        total = total + shear_taps[tap, angle, depth] * piece
    return total

def reference(slab, shear_taps, band_offsets, probe, scan_rows, scan_columns, frame_counts, amplitudes):
    margin = MAXSHIFT + TAPS
    padded_slab = jnp.pad(slab.astype(jnp.float32), ((0, 0), (0, 0), (0, 0), (margin, margin)))

    def project_angle(angle):

        def add_slice(depth, total):
            return add_taps(total, padded_slab[depth], shear_taps, band_offsets, angle, depth, 1, COLS)
        return lax.fori_loop(0, SLICES, add_slice, jnp.zeros((2, NROWS, COLS), jnp.float32))
    projection = lax.map(project_angle, jnp.arange(ANGLES, dtype=jnp.int32))
    rim = FRAME // 2
    extended = jnp.pad(projection, ((0, 0), (0, 0), (rim, rim), (0, 0)))
    anchor = jnp.zeros((), jnp.int32)

    def angle_image(angle):
        picture = extended[angle]

        def strip_step(strip, acc):
            first = (strip * CAP).astype(jnp.int32)
            row_starts = lax.dynamic_slice_in_dim(scan_rows[angle], first, CAP) + (strip * ROWS_DEV).astype(jnp.int32)
            column_starts = lax.dynamic_slice_in_dim(scan_columns[angle], first, CAP)
            measured = lax.dynamic_slice_in_dim(amplitudes[angle], first, CAP)
            live = (jnp.arange(CAP, dtype=jnp.int32) < frame_counts[angle, strip]).astype(jnp.float32)

            def cut_patch(row, column):
                return lax.dynamic_slice(picture, (anchor, row, column), (2, FRAME, FRAME))
            patches = jax.vmap(cut_patch)(row_starts, column_starts)
            gradients = frame_gradient(patches, probe, measured) * live[:, None, None, None]

            def place(which, inner):
                corner = (anchor, row_starts[which], column_starts[which])
                current = lax.dynamic_slice(inner, corner, (2, FRAME, FRAME))
                return lax.dynamic_update_slice(inner, current + gradients[which], corner)
            return lax.fori_loop(0, CAP, place, acc)
        placed = lax.fori_loop(0, STRIPS, strip_step, jnp.zeros((2, NROWS + FRAME, COLS), jnp.float32))
        return placed[:, rim:rim + NROWS].astype(jnp.bfloat16)
    image = lax.map(angle_image, jnp.arange(ANGLES, dtype=jnp.int32))
    padded_image = jnp.pad(image.astype(jnp.float32), ((0, 0), (0, 0), (0, 0), (margin, margin)))

    def back_slice(depth):

        def add_angle(angle, total):
            return add_taps(total, padded_image[angle], shear_taps, band_offsets, angle, depth, -1, COLS)
        return lax.fori_loop(0, ANGLES, add_angle, jnp.zeros((2, NROWS, COLS), jnp.float32))
    return lax.map(back_slice, jnp.arange(SLICES, dtype=jnp.int32))
```

```python
import functools
import math

import jax
import jax.numpy as jnp
import numpy as np
from jax import lax
from jax.experimental import pallas as pl
from jax.experimental.pallas import tpu as pltpu
from jax.sharding import PartitionSpec as P

MAXSHIFT = 64
LANES = 128
VMEM = pltpu.VMEM
SMEM = pltpu.SMEM


def dft_blocks(length):
    index = np.arange(length, dtype=np.int64)
    product = index[:, None] * index[None, :] % length
    phase = product.astype(np.float32) * np.float32(2.0 * math.pi / length)
    scale = np.float32(1.0 / math.sqrt(length))
    cosine = (np.cos(phase) * scale).astype(jnp.bfloat16)
    sine = (np.sin(phase) * scale).astype(jnp.bfloat16)
    forward = np.block([[cosine, sine], [-sine, cosine]])
    inverse = np.block([[cosine, -sine], [sine, cosine]])
    return forward, inverse


def lane_index(shape):
    return lax.broadcasted_iota(jnp.int32, shape, len(shape) - 1)


def shear_body(sign, taps_ref, offsets_ref, x_ref, o_ref, padded):
    count, rows, width = x_ref.shape
    tiles = width // LANES + 1
    ntaps = taps_ref.shape[0]
    left = MAXSHIFT if sign > 0 else MAXSHIFT + ntaps - 1
    step = 16

    def pad_one(s, _):
        value = x_ref[s].astype(jnp.float32)
        value = jnp.concatenate([value, jnp.zeros((rows, LANES), jnp.float32)], axis=1)
        value = pltpu.roll(value, left, axis=1)
        for j in range(tiles):
            padded[s, j] = value[:, j * LANES : (j + 1) * LANES]
        return 0

    lax.fori_loop(0, count, pad_one, 0)
    lane = lane_index((step, LANES))

    def one(d, _):
        for g in range(rows // step):
            total = [[jnp.zeros((step, LANES), jnp.float32) for _ in range(tiles)] for _ in range(ntaps)]
            for s in range(count):
                angle, depth = (d, s) if sign > 0 else (s, d)
                amount = MAXSHIFT + sign * offsets_ref[angle, depth]
                back = lax.rem(LANES - amount, LANES)
                keep = lane < LANES - amount
                turned = [pltpu.roll(padded[s, j, pl.ds(g * step, step), :], back, axis=1) for j in range(tiles)]
                moved = [jnp.where(keep, turned[j], turned[j + 1] if j + 1 < tiles else 0.0) for j in range(tiles)]
                for k in range(ntaps):
                    weight = taps_ref[k if sign > 0 else ntaps - 1 - k, angle, depth]
                    for j in range(tiles):
                        total[k][j] = total[k][j] + weight * moved[j]
            for j in range(tiles - 1):
                out = total[0][j]
                for k in range(1, ntaps):
                    here = pltpu.roll(total[k][j], LANES - k, axis=1)
                    there = pltpu.roll(total[k][j + 1], LANES - k, axis=1)
                    out = out + jnp.where(lane < LANES - k, here, there)
                o_ref[d, pl.ds(g * step, step), pl.ds(j * LANES, LANES)] = out.astype(o_ref.dtype)
        return 0

    lax.fori_loop(0, count, one, 0)


def shear(x, taps, offsets, sign):
    count, rows, width = x.shape
    return pl.pallas_call(
        functools.partial(shear_body, sign),
        out_shape=jax.ShapeDtypeStruct(x.shape, jnp.bfloat16),
        in_specs=[pl.BlockSpec(memory_space=SMEM), pl.BlockSpec(memory_space=SMEM), pl.BlockSpec(memory_space=VMEM)],
        out_specs=pl.BlockSpec(memory_space=VMEM),
        scratch_shapes=[VMEM((count, width // LANES + 1, rows, LANES), jnp.float32)],
        compiler_params=pltpu.CompilerParams(vmem_limit_bytes=16 << 20),
        name="shear_forward" if sign > 0 else "shear_back",
    )(taps, offsets, x)


def frames_body(
    odd_ref, rows_ref, columns_ref, counts_ref, own_ref, near_ref, far_ref, probe_ref, amp_ref, fwd_ref, inv_ref,
    mid_ref, to_near_ref, to_far_ref, ext, placed, column, side,
):
    length = probe_ref.shape[1]
    strip = own_ref.shape[1]
    width = own_ref.shape[2]
    chunk = 128
    odd = odd_ref[0]
    near_row = pl.multiple_of((1 - odd) * 2 * strip, strip)
    far_row = pl.multiple_of(odd * 2 * strip, strip)
    tiles = width // LANES
    for p in range(2):
        for j in range(tiles):
            tile = pl.ds(j * LANES, LANES)
            ext[p, j, pl.ds(strip, strip), :] = own_ref[p, :, tile].astype(jnp.float32)
            ext[p, j, pl.ds(near_row, strip), :] = near_ref[p, :, tile].astype(jnp.float32)
            ext[p, j, pl.ds(far_row, strip), :] = far_ref[p, :, tile].astype(jnp.float32)
    placed[...] = jnp.zeros_like(placed)
    part = 16
    lane = lane_index((part, LANES))

    def one_frame(f, _):
        row = rows_ref[0, f]
        col = columns_ref[0, f]
        first = col // LANES
        rest = lax.rem(col, LANES)
        back = lax.rem(LANES - rest, LANES)
        low = lane < LANES - rest
        high = lane >= rest

        def cut(i, _):
            at = i * part
            window = []
            for p in range(2):
                turned = [pltpu.roll(ext[p, first + j, pl.ds(row + at, part), :], back, axis=1) for j in range(3)]
                window.append([jnp.where(low, turned[j], turned[j + 1]) for j in range(2)])
            here = pl.ds(pl.multiple_of(at, part), part)
            for j in range(2):
                pr = probe_ref[0, here, pl.ds(j * LANES, LANES)].astype(jnp.float32)
                pi = probe_ref[1, here, pl.ds(j * LANES, LANES)].astype(jnp.float32)
                xr, xi = window[0][j], window[1][j]
                column[here, pl.ds(j * LANES, LANES)] = (pr * xr - pi * xi).astype(jnp.bfloat16)
                column[pl.ds(pl.multiple_of(length + at, part), part), pl.ds(j * LANES, LANES)] = (
                    pr * xi + pi * xr
                ).astype(jnp.bfloat16)
            return 0

        lax.fori_loop(0, length // part, cut, 0, unroll=4)

        def left(matrix):
            for m in range(2 * length // chunk):
                value = jnp.dot(matrix[pl.ds(m * chunk, chunk), :], column[...], preferred_element_type=jnp.float32)
                p, r = divmod(m * chunk, length)
                side[pl.ds(r, chunk), pl.ds(p * length, length)] = value.astype(jnp.bfloat16)

        left(fwd_ref)
        for m in range(length // chunk):
            here = pl.ds(m * chunk, chunk)
            far = jnp.dot(side[here, :], inv_ref[...], preferred_element_type=jnp.float32)
            fr, fi = far[:, :length], far[:, length:]
            factor = 1.0 - amp_ref[f, here, :].astype(jnp.float32) * lax.rsqrt(fr * fr + fi * fi + 1.0)
            column[here, :] = (fr * factor).astype(jnp.bfloat16)
            column[pl.ds(length + m * chunk, chunk), :] = (fi * factor).astype(jnp.bfloat16)
        left(inv_ref)
        for m in range(length // chunk):
            here = pl.ds(m * chunk, chunk)
            wave = jnp.dot(side[here, :], fwd_ref[...], preferred_element_type=jnp.float32)
            for i in range(chunk // part):
                at = m * chunk + i * part
                rs = slice(i * part, (i + 1) * part)
                turned = [[None, None], [None, None]]
                for j in range(2):
                    pr = probe_ref[0, pl.ds(at, part), pl.ds(j * LANES, LANES)].astype(jnp.float32)
                    pi = probe_ref[1, pl.ds(at, part), pl.ds(j * LANES, LANES)].astype(jnp.float32)
                    br = wave[rs, j * LANES : (j + 1) * LANES]
                    bi = wave[rs, length + j * LANES : length + (j + 1) * LANES]
                    turned[0][j] = pltpu.roll(pr * br + pi * bi, rest, axis=1)
                    turned[1][j] = pltpu.roll(pr * bi - pi * br, rest, axis=1)
                for p in range(2):
                    one, two = turned[p]
                    pieces = [jnp.where(high, one, 0.0), jnp.where(high, two, one), jnp.where(high, 0.0, two)]
                    for j in range(3):
                        spot = (p, first + j, pl.ds(row + at, part), slice(None))
                        placed[spot] = placed[spot] + pieces[j]
        return 0

    lax.fori_loop(0, counts_ref[0, 0], one_frame, 0)
    for p in range(2):
        for j in range(tiles):
            tile = pl.ds(j * LANES, LANES)
            mid_ref[p, :, tile] = placed[p, j, pl.ds(strip, strip), :]
            to_near_ref[p, :, tile] = placed[p, j, pl.ds(near_row, strip), :].astype(to_near_ref.dtype)
            to_far_ref[p, :, tile] = placed[p, j, pl.ds(far_row, strip), :].astype(to_far_ref.dtype)


def frames(odd, rows, columns, counts, own, near, far, probe, amplitudes):
    length = probe.shape[1]
    parts, strip, width = own.shape
    fwd, inv = (jnp.asarray(m) for m in dft_blocks(length))
    return pl.pallas_call(
        frames_body,
        out_shape=(
            jax.ShapeDtypeStruct(own.shape, jnp.float32),
            jax.ShapeDtypeStruct(own.shape, jnp.bfloat16),
            jax.ShapeDtypeStruct(own.shape, jnp.bfloat16),
        ),
        in_specs=[pl.BlockSpec(memory_space=SMEM)] * 4 + [pl.BlockSpec(memory_space=VMEM)] * 7,
        out_specs=(pl.BlockSpec(memory_space=VMEM),) * 3,
        scratch_shapes=[
            VMEM((parts, width // LANES + 1, 3 * strip, LANES), jnp.float32),
            VMEM((parts, width // LANES + 1, 3 * strip, LANES), jnp.float32),
            VMEM((2 * length, length), jnp.bfloat16),
            VMEM((length, 2 * length), jnp.bfloat16),
        ],
        compiler_params=pltpu.CompilerParams(vmem_limit_bytes=32 << 20),
        name="frames",
    )(odd, rows, columns, counts, own, near, far, probe, amplitudes, fwd, inv)


def per_device(slab, taps, offsets, probe, scan_rows, scan_columns, counts, amplitudes):
    parts, rows, width = slab.shape[1:]
    angles = lax.axis_size("ang")
    strips = lax.axis_size("strip")
    block = parts * rows // angles
    me = lax.axis_index("strip")

    def swap(x, partner):
        route = [(s, partner(s)) for s in range(strips) if 0 <= partner(s) < strips]
        return lax.ppermute(x, "strip", route)

    def near(x):
        return swap(x, lambda s: s ^ 1)

    def far(x):
        return swap(x, lambda s: s + 1 if s % 2 else s - 1)

    def exchange(x):
        return lax.all_to_all(x, "ang", 0, 0, tiled=True)

    mixed = exchange(slab.reshape(angles, block, width))
    projection = exchange(shear(mixed, taps, offsets, 1)).reshape(parts, rows, width)
    odd = (me & 1).astype(jnp.int32).reshape(1)
    mid, to_near, to_far = frames(
        odd, scan_rows, scan_columns, counts, projection, near(projection), far(projection), probe, amplitudes[0]
    )
    image = mid + near(to_near).astype(jnp.float32) + far(to_far).astype(jnp.float32)
    mixed = exchange(image.astype(jnp.bfloat16).reshape(angles, block, width))
    result = exchange(shear(mixed, taps, offsets, -1))
    return result.reshape(1, parts, rows, width).astype(jnp.float32)


def solution(mesh):
    return jax.shard_map(
        per_device,
        mesh=mesh,
        in_specs=(
            P("ang", None, "strip", None),
            P(),
            P(),
            P(),
            P("ang", "strip"),
            P("ang", "strip"),
            P("ang", "strip"),
            P("ang", "strip", None, None),
        ),
        out_specs=P("ang", None, "strip", None),
        check_vma=False,
    )
```

```python
import functools
import math

import jax
import jax.numpy as jnp
import numpy as np
from jax import lax
from jax.experimental import pallas as pl
from jax.experimental.pallas import tpu as pltpu
from jax.sharding import PartitionSpec as P

MAXSHIFT = 64
LANES = 128
MROWS = 256
CHUNK = 256
VMEM = pltpu.VMEM
SMEM = pltpu.SMEM


def dft_blocks(length):
    index = np.arange(length, dtype=np.int64)
    product = index[:, None] * index[None, :] % length
    phase = product.astype(np.float32) * np.float32(2.0 * math.pi / length)
    scale = np.float32(1.0 / math.sqrt(length))
    cosine = (np.cos(phase) * scale).astype(jnp.bfloat16)
    sine = (np.sin(phase) * scale).astype(jnp.bfloat16)
    forward = np.block([[cosine, sine], [-sine, cosine]])
    inverse = np.block([[cosine, -sine], [sine, cosine]])
    return forward, inverse


def in_hbm(x):
    return pltpu.with_memory_space_constraint(x, pltpu.HBM)


def lane_index(shape):
    return lax.broadcasted_iota(jnp.int32, shape, len(shape) - 1)


def shear_body(sign, taps_hbm, offsets_hbm, x_ref, o_ref, taps_ref, offsets_ref, ready, copies):
    count, rows, width = x_ref.shape
    tiles = width // LANES + 1
    ntaps = taps_ref.shape[0]
    left = MAXSHIFT if sign > 0 else MAXSHIFT + ntaps - 1
    get_taps = pltpu.make_async_copy(taps_hbm, taps_ref, ready.at[0])
    get_offsets = pltpu.make_async_copy(offsets_hbm, offsets_ref, ready.at[1])
    get_taps.start()
    get_offsets.start()

    def lay_out(s, _):
        value = x_ref[s].astype(jnp.float32)
        value = jnp.concatenate([value, jnp.zeros((rows, LANES), jnp.float32)], axis=1)
        for k in range(ntaps):
            moved = pltpu.roll(value, left - k, axis=1)
            for j in range(tiles):
                copies[s, k, j] = moved[:, j * LANES : (j + 1) * LANES]
        return 0

    lax.fori_loop(0, count, lay_out, 0)
    get_taps.wait()
    get_offsets.wait()
    lane = lane_index((rows, LANES))

    def one(d, _):
        total = [jnp.zeros((rows, LANES), jnp.float32) for _ in range(tiles - 1)]
        for s in range(count):
            angle, depth = (d, s) if sign > 0 else (s, d)
            amount = MAXSHIFT + sign * offsets_ref[angle, depth]
            back = lax.rem(LANES - amount, LANES)
            keep = lane < LANES - amount
            weights = [taps_ref[k if sign > 0 else ntaps - 1 - k, angle, depth] for k in range(ntaps)]
            turned = []
            for j in range(tiles):
                terms = [weights[k] * copies[s, k, j] for k in range(ntaps)]
                both = (terms[0] + terms[1]) + (terms[2] + terms[3])
                turned.append(pltpu.roll(both, back, axis=1))
            for j in range(tiles - 1):
                total[j] = total[j] + jnp.where(keep, turned[j], turned[j + 1])
        for j in range(tiles - 1):
            o_ref[d, :, pl.ds(j * LANES, LANES)] = total[j].astype(o_ref.dtype)
        return 0

    lax.fori_loop(0, count, one, 0)


def shear(x, taps, offsets, sign):
    count, rows, width = x.shape
    tiles = width // LANES + 1
    return pl.pallas_call(
        functools.partial(shear_body, sign),
        out_shape=jax.ShapeDtypeStruct(x.shape, jnp.bfloat16),
        in_specs=[
            pl.BlockSpec(memory_space=pltpu.HBM),
            pl.BlockSpec(memory_space=pltpu.HBM),
            pl.BlockSpec(memory_space=VMEM),
        ],
        out_specs=pl.BlockSpec(memory_space=VMEM),
        scratch_shapes=[
            SMEM(taps.shape, taps.dtype),
            SMEM(offsets.shape, offsets.dtype),
            pltpu.SemaphoreType.DMA((2,)),
            VMEM((count, taps.shape[0], tiles, rows, LANES), jnp.float32),
        ],
        compiler_params=pltpu.CompilerParams(vmem_limit_bytes=16 << 20),
        name="shear_forward" if sign > 0 else "shear_back",
    )(in_hbm(taps), in_hbm(offsets), x)


def frames_body(
    odd_ref, counts_ref, rows_hbm, columns_hbm, own_ref, near_ref, far_ref, probe_hbm, amp_ref, fwd_ref, inv_ref,
    mid_ref, to_near_ref, to_far_ref,
    ready, rows_ref, columns_ref, probe_ref, ext, placed,
    column_a, column_b, side_a, side_b, wave_a,
):
    length = probe_ref.shape[1]
    strip = own_ref.shape[1]
    width = own_ref.shape[2]
    gets = [
        pltpu.make_async_copy(src, dst, ready.at[i])
        for i, (src, dst) in enumerate(
            [(rows_hbm, rows_ref), (columns_hbm, columns_ref), (probe_hbm, probe_ref)]
        )
    ]
    for get in gets:
        get.start()
    odd = odd_ref[0]
    near_row = pl.multiple_of((1 - odd) * 2 * strip, strip)
    far_row = pl.multiple_of(odd * 2 * strip, strip)
    tiles = width // LANES
    for p in range(2):
        for j in range(tiles):
            tile = pl.ds(j * LANES, LANES)
            ext[p, j, pl.ds(strip, strip), :] = own_ref[p, :, tile].astype(jnp.float32)
            ext[p, j, pl.ds(near_row, strip), :] = near_ref[p, :, tile].astype(jnp.float32)
            ext[p, j, pl.ds(far_row, strip), :] = far_ref[p, :, tile].astype(jnp.float32)
    placed[...] = jnp.zeros_like(placed)
    wave_a[...] = jnp.zeros_like(wave_a)
    for get in gets:
        get.wait()
    part = 16
    lane = lane_index((part, LANES))
    count = counts_ref[0, 0]
    slots = amp_ref.shape[0]
    spots = range(0, length, part)

    def place_of(f):
        col = columns_ref[0, f]
        return rows_ref[0, f], col // LANES, lax.rem(col, LANES)

    def cut(f, column):
        row, first, rest = place_of(f)
        back = lax.rem(LANES - rest, LANES)
        low = lane < LANES - rest
        for at in spots:
            window = []
            for p in range(2):
                turned = [pltpu.roll(ext[p, first + j, pl.ds(row + at, part), :], back, axis=1) for j in range(3)]
                window.append([jnp.where(low, turned[j], turned[j + 1]) for j in range(2)])
            for j in range(2):
                tile = pl.ds(j * LANES, LANES)
                pr = probe_ref[0, pl.ds(at, part), tile].astype(jnp.float32)
                pi = probe_ref[1, pl.ds(at, part), tile].astype(jnp.float32)
                xr, xi = window[0][j], window[1][j]
                column[pl.ds(at, part), tile] = (pr * xr - pi * xi).astype(jnp.bfloat16)
                column[pl.ds(length + at, part), tile] = (pr * xi + pi * xr).astype(jnp.bfloat16)

    def left(matrix, column, side):
        for m in range(0, 2 * length, MROWS):
            value = jnp.dot(matrix[pl.ds(m, MROWS), :], column[...], preferred_element_type=jnp.float32)
            p, r = divmod(m, length)
            if MROWS > length:
                side[:, pl.ds(0, length)] = value[:length].astype(jnp.bfloat16)
                side[:, pl.ds(length, length)] = value[length:].astype(jnp.bfloat16)
            else:
                side[pl.ds(r, MROWS), pl.ds(p * length, length)] = value.astype(jnp.bfloat16)

    def compare(f, side, column):
        for at in spots:
            if at % CHUNK == 0:
                far = jnp.dot(side[pl.ds(at, CHUNK), :], inv_ref[...], preferred_element_type=jnp.float32)
            rs = slice(at % CHUNK, at % CHUNK + part)
            fr = far[rs, :length]
            fi = far[rs, length:]
            factor = 1.0 - amp_ref[f, pl.ds(at, part), :].astype(jnp.float32) * lax.rsqrt(fr * fr + fi * fi + 1.0)
            column[pl.ds(at, part), :] = (fr * factor).astype(jnp.bfloat16)
            column[pl.ds(length + at, part), :] = (fi * factor).astype(jnp.bfloat16)

    def turn_back(f, side, wave):
        rest = place_of(f)[2]
        for at in spots:
            if at % CHUNK == 0:
                back = jnp.dot(side[pl.ds(at, CHUNK), :], fwd_ref[...], preferred_element_type=jnp.float32)
            rs = slice(at % CHUNK, at % CHUNK + part)
            for j in range(2):
                tile = pl.ds(j * LANES, LANES)
                pr = probe_ref[0, pl.ds(at, part), tile].astype(jnp.float32)
                pi = probe_ref[1, pl.ds(at, part), tile].astype(jnp.float32)
                br = back[rs, j * LANES : (j + 1) * LANES]
                bi = back[rs, length + j * LANES : length + (j + 1) * LANES]
                wave[0, j, pl.ds(at, part), :] = pltpu.roll(pr * br + pi * bi, rest, axis=1)
                wave[1, j, pl.ds(at, part), :] = pltpu.roll(pr * bi - pi * br, rest, axis=1)

    def add(f, wave):
        row, first, rest = place_of(f)
        high = lane >= rest
        for at in spots:
            for p in range(2):
                one = wave[p, 0, pl.ds(at, part), :]
                two = wave[p, 1, pl.ds(at, part), :]
                pieces = [jnp.where(high, one, 0.0), jnp.where(high, two, one), jnp.where(high, 0.0, two)]
                for j in range(3):
                    spot = (p, first + j, pl.ds(row + at, part), slice(None))
                    placed[spot] = placed[spot] + pieces[j]

    def one_frame(f, _):
        left(fwd_ref, column_a, side_a)
        cut(jnp.minimum(f + 1, slots - 1), column_a)
        add(jnp.maximum(f - 1, 0), wave_a)
        compare(f, side_a, column_b)
        left(inv_ref, column_b, side_b)
        turn_back(f, side_b, wave_a)
        return 0

    cut(0, column_a)
    lax.fori_loop(0, count, one_frame, 0)
    add(count - 1, wave_a)
    for p in range(2):
        for j in range(tiles):
            tile = pl.ds(j * LANES, LANES)
            mid_ref[p, :, tile] = placed[p, j, pl.ds(strip, strip), :]
            to_near_ref[p, :, tile] = placed[p, j, pl.ds(near_row, strip), :].astype(to_near_ref.dtype)
            to_far_ref[p, :, tile] = placed[p, j, pl.ds(far_row, strip), :].astype(to_far_ref.dtype)


def frames(odd, rows, columns, counts, own, near, far, probe, amplitudes):
    length = probe.shape[1]
    parts, strip, width = own.shape
    fwd, inv = (jnp.asarray(m) for m in dft_blocks(length))
    hbm = pl.BlockSpec(memory_space=pltpu.HBM)
    vmem = pl.BlockSpec(memory_space=VMEM)
    return pl.pallas_call(
        frames_body,
        out_shape=(
            jax.ShapeDtypeStruct(own.shape, jnp.float32),
            jax.ShapeDtypeStruct(own.shape, jnp.bfloat16),
            jax.ShapeDtypeStruct(own.shape, jnp.bfloat16),
        ),
        in_specs=[pl.BlockSpec(memory_space=SMEM)] * 2 + [hbm] * 2 + [vmem] * 3 + [hbm] + [vmem] * 3,
        out_specs=(vmem,) * 3,
        scratch_shapes=[
            pltpu.SemaphoreType.DMA((3,)),
            SMEM(rows.shape, rows.dtype),
            SMEM(columns.shape, columns.dtype),
            VMEM(probe.shape, probe.dtype),
            VMEM((parts, width // LANES + 1, 3 * strip, LANES), jnp.float32),
            VMEM((parts, width // LANES + 1, 3 * strip, LANES), jnp.float32),
            VMEM((2 * length, length), jnp.bfloat16),
            VMEM((2 * length, length), jnp.bfloat16),
            VMEM((length, 2 * length), jnp.bfloat16),
            VMEM((length, 2 * length), jnp.bfloat16),
            VMEM((2, length // LANES, length, LANES), jnp.float32),
        ],
        compiler_params=pltpu.CompilerParams(vmem_limit_bytes=32 << 20),
        name="frames",
    )(odd, counts, in_hbm(rows), in_hbm(columns), own, near, far, in_hbm(probe), amplitudes, fwd, inv)


def per_device(slab, taps, offsets, probe, scan_rows, scan_columns, counts, amplitudes):
    parts, rows, width = slab.shape[1:]
    angles = lax.axis_size("ang")
    strips = lax.axis_size("strip")
    block = parts * rows // angles
    me = lax.axis_index("strip")

    def swap(x, partner):
        route = [(s, partner(s)) for s in range(strips) if 0 <= partner(s) < strips]
        return lax.ppermute(x, "strip", route)

    def near(x):
        return swap(x, lambda s: s ^ 1)

    def far(x):
        return swap(x, lambda s: s + 1 if s % 2 else s - 1)

    def exchange(x):
        return lax.all_to_all(x, "ang", 0, 0, tiled=True)

    mixed = exchange(slab.reshape(angles, block, width))
    projection = exchange(shear(mixed, taps, offsets, 1)).reshape(parts, rows, width)
    odd = (me & 1).astype(jnp.int32).reshape(1)
    mid, to_near, to_far = frames(
        odd, scan_rows, scan_columns, counts, projection, near(projection), far(projection), probe, amplitudes[0]
    )
    image = mid + near(to_near).astype(jnp.float32) + far(to_far).astype(jnp.float32)
    mixed = exchange(image.astype(jnp.bfloat16).reshape(angles, block, width))
    result = exchange(shear(mixed, taps, offsets, -1))
    return result.reshape(1, parts, rows, width).astype(jnp.float32)


def solution(mesh):
    return jax.shard_map(
        per_device,
        mesh=mesh,
        in_specs=(
            P("ang", None, "strip", None),
            P(),
            P(),
            P(),
            P("ang", "strip"),
            P("ang", "strip"),
            P("ang", "strip"),
            P("ang", "strip", None, None),
        ),
        out_specs=P("ang", None, "strip", None),
        check_vma=False,
    )
```

```python
import functools
import math

import jax
import jax.numpy as jnp
import numpy as np
from jax import lax
from jax.experimental import pallas as pl
from jax.experimental.pallas import tpu as pltpu
from jax.sharding import PartitionSpec as P

MAXSHIFT = 64
LANES = 128
MROWS = 256
CHUNK = 256
VMEM = pltpu.VMEM
SMEM = pltpu.SMEM


def dft_blocks(length):
    index = np.arange(length, dtype=np.int64)
    product = index[:, None] * index[None, :] % length
    phase = product.astype(np.float32) * np.float32(2.0 * math.pi / length)
    scale = np.float32(1.0 / math.sqrt(length))
    cosine = (np.cos(phase) * scale).astype(jnp.bfloat16)
    sine = (np.sin(phase) * scale).astype(jnp.bfloat16)
    forward = np.block([[cosine, sine], [-sine, cosine]])
    inverse = np.block([[cosine, -sine], [sine, cosine]])
    return forward, inverse


def in_hbm(x):
    return pltpu.with_memory_space_constraint(x, pltpu.HBM)


def lane_index(shape):
    return lax.broadcasted_iota(jnp.int32, shape, len(shape) - 1)


def shear_body(sign, taps_hbm, offsets_hbm, x_ref, o_ref, taps_ref, offsets_ref, ready, copies):
    count = taps_ref.shape[1]
    rows, width = x_ref.shape[1:]
    tiles = width // LANES + 1
    ntaps = taps_ref.shape[0]
    left = MAXSHIFT if sign > 0 else MAXSHIFT + ntaps - 1
    get_taps = pltpu.make_async_copy(taps_hbm, taps_ref, ready.at[0])
    get_offsets = pltpu.make_async_copy(offsets_hbm, offsets_ref, ready.at[1])
    get_taps.start()
    get_offsets.start()

    def lay_out(s, _):
        value = x_ref[s].astype(jnp.float32)
        for again in range(1, x_ref.shape[0] // count):
            value = value + x_ref[s + again * count].astype(jnp.float32)
        value = jnp.concatenate([value, jnp.zeros((rows, LANES), jnp.float32)], axis=1)
        for k in range(ntaps):
            moved = pltpu.roll(value, left - k, axis=1)
            for j in range(tiles):
                copies[s, k, j] = moved[:, j * LANES : (j + 1) * LANES]
        return 0

    lax.fori_loop(0, count, lay_out, 0)
    get_taps.wait()
    get_offsets.wait()
    lane = lane_index((rows, LANES))

    def one(d, _):
        total = [jnp.zeros((rows, LANES), jnp.float32) for _ in range(tiles - 1)]
        for s in range(count):
            angle, depth = (d, s) if sign > 0 else (s, d)
            amount = MAXSHIFT + sign * offsets_ref[angle, depth]
            back = lax.rem(LANES - amount, LANES)
            keep = lane < LANES - amount
            weights = [taps_ref[k if sign > 0 else ntaps - 1 - k, angle, depth] for k in range(ntaps)]
            turned = []
            for j in range(tiles):
                terms = [weights[k] * copies[s, k, j] for k in range(ntaps)]
                both = (terms[0] + terms[1]) + (terms[2] + terms[3])
                turned.append(pltpu.roll(both, back, axis=1))
            for j in range(tiles - 1):
                total[j] = total[j] + jnp.where(keep, turned[j], turned[j + 1])
        for j in range(tiles - 1):
            out = total[j].astype(o_ref.dtype)
            for again in range(o_ref.shape[0] // count):
                o_ref[d + again * count, :, pl.ds(j * LANES, LANES)] = out
        return 0

    lax.fori_loop(0, count, one, 0)


def shear(x, taps, offsets, sign, copies):
    rows, width = x.shape[1:]
    count = taps.shape[1]
    tiles = width // LANES + 1
    return pl.pallas_call(
        functools.partial(shear_body, sign),
        out_shape=jax.ShapeDtypeStruct((copies * count, rows, width), jnp.bfloat16),
        in_specs=[
            pl.BlockSpec(memory_space=pltpu.HBM),
            pl.BlockSpec(memory_space=pltpu.HBM),
            pl.BlockSpec(memory_space=VMEM),
        ],
        out_specs=pl.BlockSpec(memory_space=VMEM),
        scratch_shapes=[
            SMEM(taps.shape, taps.dtype),
            SMEM(offsets.shape, offsets.dtype),
            pltpu.SemaphoreType.DMA((2,)),
            VMEM((count, taps.shape[0], tiles, rows, LANES), jnp.float32),
        ],
        compiler_params=pltpu.CompilerParams(vmem_limit_bytes=16 << 20),
        name="shear_forward" if sign > 0 else "shear_back",
    )(in_hbm(taps), in_hbm(offsets), x)


def frames_body(
    place_ref, counts_ref, rows_hbm, columns_hbm, pair_ref, near_ref, probe_hbm, fwd_hbm, inv_hbm, amp_hbm,
    mid_ref, to_near_ref, send_ref,
    ready, rows_ref, columns_ref, probe_ref, fwd_ref, inv_ref, amp_ref, ext, placed,
    column_a, column_b, side_a, side_b, wave_a,
):
    length = probe_ref.shape[1]
    strip, width = near_ref.shape[1:]
    pairs = [
        (rows_hbm, rows_ref),
        (columns_hbm, columns_ref),
        (probe_hbm, probe_ref),
        (fwd_hbm, fwd_ref),
        (inv_hbm, inv_ref),
        (amp_hbm, amp_ref),
    ]
    gets = [pltpu.make_async_copy(src, dst, ready.at[i]) for i, (src, dst) in enumerate(pairs)]
    for get in gets:
        get.start()
    odd = place_ref[0]
    has_far = place_ref[1] > 0
    near_row = pl.multiple_of((1 - odd) * 2 * strip, strip)
    far_row = pl.multiple_of(odd * 2 * strip, strip)
    tiles = width // LANES
    for p in range(2):
        for j in range(tiles):
            tile = pl.ds(j * LANES, LANES)
            ext[p, j, pl.ds(strip, strip), :] = pair_ref[1 - odd, p, :, tile].astype(jnp.float32)
            ext[p, j, pl.ds(near_row, strip), :] = near_ref[p, :, tile].astype(jnp.float32)
            far = pair_ref[odd, p, :, tile].astype(jnp.float32)
            ext[p, j, pl.ds(far_row, strip), :] = jnp.where(has_far, far, 0.0)
    placed[...] = jnp.zeros_like(placed)
    wave_a[...] = jnp.zeros_like(wave_a)
    for get in gets[:3]:
        get.wait()
    part = 16
    lane = lane_index((part, LANES))
    count = counts_ref[0, 0]
    slots = amp_ref.shape[0]
    spots = range(0, length, part)

    def place_of(f):
        col = columns_ref[0, f]
        return rows_ref[0, f], col // LANES, lax.rem(col, LANES)

    def cut(f, column):
        row, first, rest = place_of(f)
        back = lax.rem(LANES - rest, LANES)
        low = lane < LANES - rest
        for at in spots:
            window = []
            for p in range(2):
                turned = [pltpu.roll(ext[p, first + j, pl.ds(row + at, part), :], back, axis=1) for j in range(3)]
                window.append([jnp.where(low, turned[j], turned[j + 1]) for j in range(2)])
            for j in range(2):
                tile = pl.ds(j * LANES, LANES)
                pr = probe_ref[0, pl.ds(at, part), tile].astype(jnp.float32)
                pi = probe_ref[1, pl.ds(at, part), tile].astype(jnp.float32)
                xr, xi = window[0][j], window[1][j]
                column[pl.ds(at, part), tile] = (pr * xr - pi * xi).astype(jnp.bfloat16)
                column[pl.ds(length + at, part), tile] = (pr * xi + pi * xr).astype(jnp.bfloat16)

    def left(matrix, column, side):
        for m in range(0, 2 * length, MROWS):
            value = jnp.dot(matrix[pl.ds(m, MROWS), :], column[...], preferred_element_type=jnp.float32)
            p, r = divmod(m, length)
            if MROWS > length:
                side[:, pl.ds(0, length)] = value[:length].astype(jnp.bfloat16)
                side[:, pl.ds(length, length)] = value[length:].astype(jnp.bfloat16)
            else:
                side[pl.ds(r, MROWS), pl.ds(p * length, length)] = value.astype(jnp.bfloat16)

    def compare(f, side, column):
        for at in spots:
            if at % CHUNK == 0:
                far = jnp.dot(side[pl.ds(at, CHUNK), :], inv_ref[...], preferred_element_type=jnp.float32)
            rs = slice(at % CHUNK, at % CHUNK + part)
            fr = far[rs, :length]
            fi = far[rs, length:]
            factor = 1.0 - amp_ref[f, pl.ds(at, part), :].astype(jnp.float32) * lax.rsqrt(fr * fr + fi * fi + 1.0)
            column[pl.ds(at, part), :] = (fr * factor).astype(jnp.bfloat16)
            column[pl.ds(length + at, part), :] = (fi * factor).astype(jnp.bfloat16)

    def turn_back(f, side, wave):
        rest = place_of(f)[2]
        for at in spots:
            if at % CHUNK == 0:
                back = jnp.dot(side[pl.ds(at, CHUNK), :], fwd_ref[...], preferred_element_type=jnp.float32)
            rs = slice(at % CHUNK, at % CHUNK + part)
            for j in range(2):
                tile = pl.ds(j * LANES, LANES)
                pr = probe_ref[0, pl.ds(at, part), tile].astype(jnp.float32)
                pi = probe_ref[1, pl.ds(at, part), tile].astype(jnp.float32)
                br = back[rs, j * LANES : (j + 1) * LANES]
                bi = back[rs, length + j * LANES : length + (j + 1) * LANES]
                wave[0, j, pl.ds(at, part), :] = pltpu.roll(pr * br + pi * bi, rest, axis=1)
                wave[1, j, pl.ds(at, part), :] = pltpu.roll(pr * bi - pi * br, rest, axis=1)

    def add(f, wave):
        row, first, rest = place_of(f)
        high = lane >= rest
        for at in spots:
            for p in range(2):
                one = wave[p, 0, pl.ds(at, part), :]
                two = wave[p, 1, pl.ds(at, part), :]
                pieces = [jnp.where(high, one, 0.0), jnp.where(high, two, one), jnp.where(high, 0.0, two)]
                for j in range(3):
                    spot = (p, first + j, pl.ds(row + at, part), slice(None))
                    placed[spot] = placed[spot] + pieces[j]

    def one_frame(f, _):
        left(fwd_ref, column_a, side_a)
        cut(jnp.minimum(f + 1, slots - 1), column_a)
        add(jnp.maximum(f - 1, 0), wave_a)
        compare(f, side_a, column_b)
        left(inv_ref, column_b, side_b)
        turn_back(f, side_b, wave_a)
        return 0

    cut(0, column_a)
    for get in gets[3:]:
        get.wait()
    lax.fori_loop(0, count, one_frame, 0)
    add(count - 1, wave_a)
    for p in range(2):
        for j in range(tiles):
            tile = pl.ds(j * LANES, LANES)
            mid_ref[p, :, tile] = placed[p, j, pl.ds(strip, strip), :]
            to_near_ref[p, :, tile] = placed[p, j, pl.ds(near_row, strip), :].astype(to_near_ref.dtype)
            far = jnp.where(has_far, placed[p, j, pl.ds(far_row, strip), :], 0.0)
            send_ref[odd, p, :, tile] = far.astype(send_ref.dtype)


def frames(place, counts, rows, columns, pair, near, probe, amplitudes):
    length = probe.shape[1]
    parts, strip, width = near.shape
    fwd, inv = (jnp.asarray(m) for m in dft_blocks(length))
    smem = pl.BlockSpec(memory_space=SMEM)
    hbm = pl.BlockSpec(memory_space=pltpu.HBM)
    vmem = pl.BlockSpec(memory_space=VMEM)
    return pl.pallas_call(
        frames_body,
        out_shape=(
            jax.ShapeDtypeStruct(near.shape, jnp.float32),
            jax.ShapeDtypeStruct(near.shape, jnp.bfloat16),
            jax.ShapeDtypeStruct(pair.shape, jnp.bfloat16),
        ),
        in_specs=[smem] * 2 + [hbm] * 2 + [vmem] * 2 + [hbm] * 4,
        out_specs=(vmem,) * 3,
        scratch_shapes=[
            pltpu.SemaphoreType.DMA((6,)),
            SMEM(rows.shape, rows.dtype),
            SMEM(columns.shape, columns.dtype),
            VMEM(probe.shape, probe.dtype),
            VMEM(fwd.shape, fwd.dtype),
            VMEM(inv.shape, inv.dtype),
            VMEM(amplitudes.shape, amplitudes.dtype),
            VMEM((parts, width // LANES + 1, 3 * strip, LANES), jnp.float32),
            VMEM((parts, width // LANES + 1, 3 * strip, LANES), jnp.float32),
            VMEM((2 * length, length), jnp.bfloat16),
            VMEM((2 * length, length), jnp.bfloat16),
            VMEM((length, 2 * length), jnp.bfloat16),
            VMEM((length, 2 * length), jnp.bfloat16),
            VMEM((2, length // LANES, length, LANES), jnp.float32),
        ],
        compiler_params=pltpu.CompilerParams(vmem_limit_bytes=32 << 20),
        name="frames",
    )(place, counts, in_hbm(rows), in_hbm(columns), pair, near, in_hbm(probe), in_hbm(fwd), in_hbm(inv), in_hbm(amplitudes))


def per_device(slab, taps, offsets, probe, scan_rows, scan_columns, counts, amplitudes):
    parts, rows, width = slab.shape[1:]
    angles = lax.axis_size("ang")
    strips = lax.axis_size("strip")
    block = parts * rows // angles
    me = lax.axis_index("strip")
    odd = (me & 1).astype(jnp.int32)
    has_far = ((me > 0) & (me < strips - 1)).astype(jnp.int32)
    groups = [
        [a * strips + s % strips for s in (first, first + 1) for a in range(angles)] for first in range(1, strips, 2)
    ]

    def swap(x):
        return lax.ppermute(x, "strip", [(s, s ^ 1) for s in range(strips)])

    def exchange(x):
        return lax.all_to_all(x, "ang", 0, 0, tiled=True)

    def pair_exchange(x):
        return lax.all_to_all(x, ("ang", "strip"), 0, 0, axis_index_groups=groups, tiled=True)

    mixed = exchange(slab.reshape(angles, block, width))
    pair = pair_exchange(shear(mixed, taps, offsets, 1, 2)).reshape(2, parts, rows, width)
    near = swap(lax.dynamic_index_in_dim(pair, 1 - odd, 0, keepdims=False))
    place = jnp.stack([odd, has_far])
    mid, to_near, send = frames(place, counts, scan_rows, scan_columns, pair, near, probe, amplitudes[0])
    own = (mid + swap(to_near).astype(jnp.float32)).astype(jnp.bfloat16)
    send = lax.dynamic_update_index_in_dim(send, own, 1 - odd, 0)
    mixed = pair_exchange(send.reshape(2 * angles, block, width))
    result = exchange(shear(mixed, taps, offsets, -1, 1))
    return result.reshape(1, parts, rows, width).astype(jnp.float32)


def solution(mesh):
    return jax.shard_map(
        per_device,
        mesh=mesh,
        in_specs=(
            P("ang", None, "strip", None),
            P(),
            P(),
            P(),
            P("ang", "strip"),
            P("ang", "strip"),
            P("ang", "strip"),
            P("ang", "strip", None, None),
        ),
        out_specs=P("ang", None, "strip", None),
        check_vma=False,
    )
```

```python
import functools
import math

import jax
import jax.numpy as jnp
import numpy as np
from jax import lax
from jax.experimental import pallas as pl
from jax.experimental.pallas import tpu as pltpu
from jax.sharding import PartitionSpec as P

MAXSHIFT = 64
LANES = 128
MROWS = 256
CHUNK = 256
VMEM = pltpu.VMEM
SMEM = pltpu.SMEM


def dft_blocks(length):
    index = np.arange(length, dtype=np.int64)
    product = index[:, None] * index[None, :] % length
    phase = product.astype(np.float32) * np.float32(2.0 * math.pi / length)
    scale = np.float32(1.0 / math.sqrt(length))
    cosine = (np.cos(phase) * scale).astype(jnp.bfloat16)
    sine = (np.sin(phase) * scale).astype(jnp.bfloat16)
    forward = np.block([[cosine, sine], [-sine, cosine]])
    inverse = np.block([[cosine, -sine], [sine, cosine]])
    return forward, inverse


def in_hbm(x):
    return pltpu.with_memory_space_constraint(x, pltpu.HBM)


def lane_index(shape):
    return lax.broadcasted_iota(jnp.int32, shape, len(shape) - 1)


def shear_body(sign, ahead, taps_hbm, offsets_hbm, x_ref, *refs):
    o_ref, taps_ref, offsets_ref, ready, copies = refs[ahead:]
    count = taps_ref.shape[1]
    rows, width = x_ref.shape[1:]
    tiles = width // LANES + 1
    ntaps = taps_ref.shape[0]
    left = MAXSHIFT if sign > 0 else MAXSHIFT + ntaps - 1
    get_taps = pltpu.make_async_copy(taps_hbm, taps_ref, ready.at[0])
    get_offsets = pltpu.make_async_copy(offsets_hbm, offsets_ref, ready.at[1])
    get_taps.start()
    get_offsets.start()

    def lay_out(s, _):
        value = x_ref[s].astype(jnp.float32)
        for again in range(1, x_ref.shape[0] // count):
            value = value + x_ref[s + again * count].astype(jnp.float32)
        value = jnp.concatenate([value, jnp.zeros((rows, LANES), jnp.float32)], axis=1)
        for k in range(ntaps):
            moved = pltpu.roll(value, left - k, axis=1)
            for j in range(tiles):
                copies[s, k, j] = moved[:, j * LANES : (j + 1) * LANES]
        return 0

    lax.fori_loop(0, count, lay_out, 0)
    get_taps.wait()
    get_offsets.wait()
    lane = lane_index((rows, LANES))

    def one(d, _):
        total = [jnp.zeros((rows, LANES), jnp.float32) for _ in range(tiles - 1)]
        for s in range(count):
            angle, depth = (d, s) if sign > 0 else (s, d)
            amount = MAXSHIFT + sign * offsets_ref[angle, depth]
            back = lax.rem(LANES - amount, LANES)
            keep = lane < LANES - amount
            weights = [taps_ref[k if sign > 0 else ntaps - 1 - k, angle, depth] for k in range(ntaps)]
            turned = []
            for j in range(tiles):
                terms = [weights[k] * copies[s, k, j] for k in range(ntaps)]
                both = (terms[0] + terms[1]) + (terms[2] + terms[3])
                turned.append(pltpu.roll(both, back, axis=1))
            for j in range(tiles - 1):
                total[j] = total[j] + jnp.where(keep, turned[j], turned[j + 1])
        for j in range(tiles - 1):
            out = total[j].astype(o_ref.dtype)
            for again in range(o_ref.shape[0] // count):
                o_ref[d + again * count, :, pl.ds(j * LANES, LANES)] = out
        return 0

    lax.fori_loop(0, count, one, 0)


def shear(x, taps, offsets, sign, copies, *ahead):
    rows, width = x.shape[1:]
    count = taps.shape[1]
    tiles = width // LANES + 1
    return pl.pallas_call(
        functools.partial(shear_body, sign, len(ahead)),
        out_shape=jax.ShapeDtypeStruct((copies * count, rows, width), jnp.bfloat16),
        in_specs=[
            pl.BlockSpec(memory_space=pltpu.HBM),
            pl.BlockSpec(memory_space=pltpu.HBM),
            pl.BlockSpec(memory_space=VMEM),
        ]
        + [pl.BlockSpec(memory_space=SMEM)] * len(ahead),
        out_specs=pl.BlockSpec(memory_space=VMEM),
        scratch_shapes=[
            SMEM(taps.shape, taps.dtype),
            SMEM(offsets.shape, offsets.dtype),
            pltpu.SemaphoreType.DMA((2,)),
            VMEM((count, taps.shape[0], tiles, rows, LANES), jnp.float32),
        ],
        compiler_params=pltpu.CompilerParams(vmem_limit_bytes=16 << 20),
        name="shear_forward" if sign > 0 else "shear_back",
    )(in_hbm(taps), in_hbm(offsets), x, *ahead)


def frames_body(
    strips, strip_ref, counts_ref, rows_hbm, columns_hbm, pair_ref, near_ref, probe_hbm, fwd_ref, inv_ref, amp_ref,
    mid_ref, to_near_ref, send_ref,
    ready, rows_ref, columns_ref, probe_ref, ext, placed,
    column_a, column_b, side_a, side_b, wave_a,
):
    length = probe_ref.shape[1]
    strip, width = near_ref.shape[1:]
    pairs = [
        (rows_hbm, rows_ref),
        (columns_hbm, columns_ref),
        (probe_hbm, probe_ref),
    ]
    gets = [pltpu.make_async_copy(src, dst, ready.at[i]) for i, (src, dst) in enumerate(pairs)]
    for get in gets:
        get.start()
    me = strip_ref[0]
    odd = me & 1
    has_far = (me > 0) & (me < strips - 1)
    near_row = pl.multiple_of((1 - odd) * 2 * strip, strip)
    far_row = pl.multiple_of(odd * 2 * strip, strip)
    tiles = width // LANES
    for p in range(2):
        for j in range(tiles):
            tile = pl.ds(j * LANES, LANES)
            ext[p, j, pl.ds(strip, strip), :] = pair_ref[1 - odd, p, :, tile].astype(jnp.float32)
            ext[p, j, pl.ds(near_row, strip), :] = near_ref[p, :, tile].astype(jnp.float32)
            far = pair_ref[odd, p, :, tile].astype(jnp.float32)
            ext[p, j, pl.ds(far_row, strip), :] = jnp.where(has_far, far, 0.0)
    placed[...] = jnp.zeros_like(placed)
    wave_a[...] = jnp.zeros_like(wave_a)
    for get in gets:
        get.wait()
    part = 16
    lane = lane_index((part, LANES))
    count = counts_ref[0, 0]
    slots = amp_ref.shape[0]
    spots = range(0, length, part)

    def place_of(f):
        col = columns_ref[0, f]
        return rows_ref[0, f], col // LANES, lax.rem(col, LANES)

    def cut(f, column):
        row, first, rest = place_of(f)
        back = lax.rem(LANES - rest, LANES)
        low = lane < LANES - rest
        for at in spots:
            window = []
            for p in range(2):
                turned = [pltpu.roll(ext[p, first + j, pl.ds(row + at, part), :], back, axis=1) for j in range(3)]
                window.append([jnp.where(low, turned[j], turned[j + 1]) for j in range(2)])
            for j in range(2):
                tile = pl.ds(j * LANES, LANES)
                pr = probe_ref[0, pl.ds(at, part), tile].astype(jnp.float32)
                pi = probe_ref[1, pl.ds(at, part), tile].astype(jnp.float32)
                xr, xi = window[0][j], window[1][j]
                column[pl.ds(at, part), tile] = (pr * xr - pi * xi).astype(jnp.bfloat16)
                column[pl.ds(length + at, part), tile] = (pr * xi + pi * xr).astype(jnp.bfloat16)

    def left(matrix, column, side):
        for m in range(0, 2 * length, MROWS):
            value = jnp.dot(matrix[pl.ds(m, MROWS), :], column[...], preferred_element_type=jnp.float32)
            p, r = divmod(m, length)
            if MROWS > length:
                side[:, pl.ds(0, length)] = value[:length].astype(jnp.bfloat16)
                side[:, pl.ds(length, length)] = value[length:].astype(jnp.bfloat16)
            else:
                side[pl.ds(r, MROWS), pl.ds(p * length, length)] = value.astype(jnp.bfloat16)

    def compare(f, side, column):
        for at in spots:
            if at % CHUNK == 0:
                far = jnp.dot(side[pl.ds(at, CHUNK), :], inv_ref[...], preferred_element_type=jnp.float32)
            rs = slice(at % CHUNK, at % CHUNK + part)
            fr = far[rs, :length]
            fi = far[rs, length:]
            factor = 1.0 - amp_ref[f, pl.ds(at, part), :].astype(jnp.float32) * lax.rsqrt(fr * fr + fi * fi + 1.0)
            column[pl.ds(at, part), :] = (fr * factor).astype(jnp.bfloat16)
            column[pl.ds(length + at, part), :] = (fi * factor).astype(jnp.bfloat16)

    def turn_back(f, side, wave):
        rest = place_of(f)[2]
        for at in spots:
            if at % CHUNK == 0:
                back = jnp.dot(side[pl.ds(at, CHUNK), :], fwd_ref[...], preferred_element_type=jnp.float32)
            rs = slice(at % CHUNK, at % CHUNK + part)
            for j in range(2):
                tile = pl.ds(j * LANES, LANES)
                pr = probe_ref[0, pl.ds(at, part), tile].astype(jnp.float32)
                pi = probe_ref[1, pl.ds(at, part), tile].astype(jnp.float32)
                br = back[rs, j * LANES : (j + 1) * LANES]
                bi = back[rs, length + j * LANES : length + (j + 1) * LANES]
                wave[0, j, pl.ds(at, part), :] = pltpu.roll(pr * br + pi * bi, rest, axis=1)
                wave[1, j, pl.ds(at, part), :] = pltpu.roll(pr * bi - pi * br, rest, axis=1)

    def add(f, wave):
        row, first, rest = place_of(f)
        high = lane >= rest
        for at in spots:
            for p in range(2):
                one = wave[p, 0, pl.ds(at, part), :]
                two = wave[p, 1, pl.ds(at, part), :]
                pieces = [jnp.where(high, one, 0.0), jnp.where(high, two, one), jnp.where(high, 0.0, two)]
                for j in range(3):
                    spot = (p, first + j, pl.ds(row + at, part), slice(None))
                    placed[spot] = placed[spot] + pieces[j]

    def one_frame(f, _):
        left(fwd_ref, column_a, side_a)
        cut(jnp.minimum(f + 1, slots - 1), column_a)
        add(jnp.maximum(f - 1, 0), wave_a)
        compare(f, side_a, column_b)
        left(inv_ref, column_b, side_b)
        turn_back(f, side_b, wave_a)
        return 0

    cut(0, column_a)
    lax.fori_loop(0, count, one_frame, 0)
    add(count - 1, wave_a)
    for p in range(2):
        for j in range(tiles):
            tile = pl.ds(j * LANES, LANES)
            mid_ref[p, :, tile] = placed[p, j, pl.ds(strip, strip), :]
            to_near_ref[p, :, tile] = placed[p, j, pl.ds(near_row, strip), :].astype(to_near_ref.dtype)
            far = jnp.where(has_far, placed[p, j, pl.ds(far_row, strip), :], 0.0)
            send_ref[odd, p, :, tile] = far.astype(send_ref.dtype)


def frames(me, strips, counts, rows, columns, pair, near, probe, amplitudes):
    length = probe.shape[1]
    parts, strip, width = near.shape
    fwd, inv = (jnp.asarray(m) for m in dft_blocks(length))
    smem = pl.BlockSpec(memory_space=SMEM)
    hbm = pl.BlockSpec(memory_space=pltpu.HBM)
    vmem = pl.BlockSpec(memory_space=VMEM)
    return pl.pallas_call(
        functools.partial(frames_body, strips),
        out_shape=(
            jax.ShapeDtypeStruct(near.shape, jnp.float32),
            jax.ShapeDtypeStruct(near.shape, jnp.bfloat16),
            jax.ShapeDtypeStruct(pair.shape, jnp.bfloat16),
        ),
        in_specs=[smem] * 2 + [hbm] * 2 + [vmem] * 2 + [hbm] + [vmem] * 3,
        out_specs=(vmem,) * 3,
        scratch_shapes=[
            pltpu.SemaphoreType.DMA((3,)),
            SMEM(rows.shape, rows.dtype),
            SMEM(columns.shape, columns.dtype),
            VMEM(probe.shape, probe.dtype),
            VMEM((parts, width // LANES + 1, 3 * strip, LANES), jnp.float32),
            VMEM((parts, width // LANES + 1, 3 * strip, LANES), jnp.float32),
            VMEM((2 * length, length), jnp.bfloat16),
            VMEM((2 * length, length), jnp.bfloat16),
            VMEM((length, 2 * length), jnp.bfloat16),
            VMEM((length, 2 * length), jnp.bfloat16),
            VMEM((2, length // LANES, length, LANES), jnp.float32),
        ],
        compiler_params=pltpu.CompilerParams(vmem_limit_bytes=32 << 20),
        name="frames",
    )(me, counts, in_hbm(rows), in_hbm(columns), pair, near, in_hbm(probe), fwd, inv, amplitudes)


def per_device(slab, taps, offsets, probe, scan_rows, scan_columns, counts, amplitudes):
    parts, rows, width = slab.shape[1:]
    angles = lax.axis_size("ang")
    strips = lax.axis_size("strip")
    block = parts * rows // angles
    me = lax.axis_index("strip")
    own_half = (me.astype(jnp.uint32) & 1) ^ 1
    place, half = me.astype(jnp.int32).reshape(1), own_half.astype(jnp.int32).reshape(1)
    groups = [
        [a * strips + s % strips for s in (first, first + 1) for a in range(angles)] for first in range(1, strips, 2)
    ]

    def swap(x):
        return lax.ppermute(x, "strip", [(s, s ^ 1) for s in range(strips)])

    def exchange(x):
        return lax.all_to_all(x, "ang", 0, 0, tiled=True)

    def pair_exchange(x):
        return lax.all_to_all(x, ("ang", "strip"), 0, 0, axis_index_groups=groups, tiled=True)

    mixed = exchange(slab.reshape(angles, block, width))
    pair = pair_exchange(shear(mixed, taps, offsets, 1, 2, place, half)).reshape(2, parts, rows, width)
    near = swap(lax.dynamic_index_in_dim(pair, own_half, 0, keepdims=False))
    mid, to_near, send = frames(place, strips, counts, scan_rows, scan_columns, pair, near, probe, amplitudes[0])
    own = (mid + swap(to_near).astype(jnp.float32)).astype(jnp.bfloat16)
    send = lax.dynamic_update_index_in_dim(send, own, own_half, 0)
    mixed = pair_exchange(send.reshape(2 * angles, block, width))
    result = exchange(shear(mixed, taps, offsets, -1, 1))
    return result.reshape(1, parts, rows, width).astype(jnp.float32)


def solution(mesh):
    return jax.shard_map(
        per_device,
        mesh=mesh,
        in_specs=(
            P("ang", None, "strip", None),
            P(),
            P(),
            P(),
            P("ang", "strip"),
            P("ang", "strip"),
            P("ang", "strip"),
            P("ang", "strip", None, None),
        ),
        out_specs=P("ang", None, "strip", None),
        check_vma=False,
    )
```

```python
import functools
import math

import jax
import jax.numpy as jnp
import numpy as np
from jax import lax
from jax.experimental import pallas as pl
from jax.experimental.pallas import tpu as pltpu
from jax.sharding import PartitionSpec as P

MAXSHIFT = 64
LANES = 128
MROWS = 256
CHUNK = 256
VMEM = pltpu.VMEM
SMEM = pltpu.SMEM


def dft_blocks(length):
    index = np.arange(length, dtype=np.int64)
    product = index[:, None] * index[None, :] % length
    phase = product.astype(np.float32) * np.float32(2.0 * math.pi / length)
    scale = np.float32(1.0 / math.sqrt(length))
    cosine = (np.cos(phase) * scale).astype(jnp.bfloat16)
    sine = (np.sin(phase) * scale).astype(jnp.bfloat16)
    forward = np.block([[cosine, sine], [-sine, cosine]])
    inverse = np.block([[cosine, -sine], [sine, cosine]])
    return forward, inverse


def in_hbm(x):
    return pltpu.with_memory_space_constraint(x, pltpu.HBM)


def lane_index(shape):
    return lax.broadcasted_iota(jnp.int32, shape, len(shape) - 1)


def shear_body(sign, ahead, taps_hbm, offsets_hbm, x_ref, *refs):
    o_ref, taps_ref, offsets_ref, ready, copies = refs[ahead:]
    count = taps_ref.shape[1]
    rows, width = x_ref.shape[1:]
    tiles = width // LANES + 1
    ntaps = taps_ref.shape[0]
    left = MAXSHIFT if sign > 0 else MAXSHIFT + ntaps - 1
    get_taps = pltpu.make_async_copy(taps_hbm, taps_ref, ready.at[0])
    get_offsets = pltpu.make_async_copy(offsets_hbm, offsets_ref, ready.at[1])
    get_taps.start()
    get_offsets.start()

    def lay_out(s, _):
        value = x_ref[s].astype(jnp.float32)
        for again in range(1, x_ref.shape[0] // count):
            value = value + x_ref[s + again * count].astype(jnp.float32)
        value = value.astype(jnp.bfloat16).astype(jnp.float32)
        value = jnp.concatenate([value, jnp.zeros((rows, LANES), jnp.float32)], axis=1)
        for k in range(ntaps):
            moved = pltpu.roll(value, left - k, axis=1)
            for j in range(tiles):
                copies[s, k, j] = moved[:, j * LANES : (j + 1) * LANES]
        return 0

    lax.fori_loop(0, count, lay_out, 0, unroll=4)
    get_taps.wait()
    get_offsets.wait()
    lane = lane_index((rows, LANES))

    def one(d, _):
        total = [jnp.zeros((rows, LANES), jnp.float32) for _ in range(tiles - 1)]
        for s in range(count):
            angle, depth = (d, s) if sign > 0 else (s, d)
            amount = MAXSHIFT + sign * offsets_ref[angle, depth]
            back = lax.rem(LANES - amount, LANES)
            keep = lane < LANES - amount
            weights = [taps_ref[k if sign > 0 else ntaps - 1 - k, angle, depth] for k in range(ntaps)]
            turned = []
            for j in range(tiles):
                terms = [weights[k] * copies[s, k, j] for k in range(ntaps)]
                both = (terms[0] + terms[1]) + (terms[2] + terms[3])
                turned.append(pltpu.roll(both, back, axis=1))
            for j in range(tiles - 1):
                total[j] = total[j] + jnp.where(keep, turned[j], turned[j + 1])
        for j in range(tiles - 1):
            out = total[j].astype(o_ref.dtype)
            for again in range(o_ref.shape[0] // count):
                o_ref[d + again * count, :, pl.ds(j * LANES, LANES)] = out
        return 0

    lax.fori_loop(0, count, one, 0, unroll=4)


def shear(x, taps, offsets, sign, copies, *ahead):
    rows, width = x.shape[1:]
    count = taps.shape[1]
    tiles = width // LANES + 1
    return pl.pallas_call(
        functools.partial(shear_body, sign, len(ahead)),
        out_shape=jax.ShapeDtypeStruct((copies * count, rows, width), jnp.bfloat16),
        in_specs=[
            pl.BlockSpec(memory_space=pltpu.HBM),
            pl.BlockSpec(memory_space=pltpu.HBM),
            pl.BlockSpec(memory_space=VMEM),
        ]
        + [pl.BlockSpec(memory_space=SMEM)] * len(ahead),
        out_specs=pl.BlockSpec(memory_space=VMEM),
        scratch_shapes=[
            SMEM(taps.shape, taps.dtype),
            SMEM(offsets.shape, offsets.dtype),
            pltpu.SemaphoreType.DMA((2,)),
            VMEM((count, taps.shape[0], tiles, rows, LANES), jnp.float32),
        ],
        compiler_params=pltpu.CompilerParams(vmem_limit_bytes=16 << 20),
        name="shear_forward" if sign > 0 else "shear_back",
    )(in_hbm(taps), in_hbm(offsets), x, *ahead)


def frames_body(
    strips, strip_ref, counts_ref, rows_hbm, columns_hbm, pair_ref, near_ref, probe_hbm, fwd_ref, inv_ref, amp_ref,
    mid_ref, to_near_ref, send_ref,
    ready, rows_ref, columns_ref, probe_ref, ext, placed,
    column_a, column_b, side_a, side_b, wave_a,
):
    length = probe_ref.shape[1]
    strip, width = near_ref.shape[1:]
    pairs = [
        (rows_hbm, rows_ref),
        (columns_hbm, columns_ref),
        (probe_hbm, probe_ref),
    ]
    gets = [pltpu.make_async_copy(src, dst, ready.at[i]) for i, (src, dst) in enumerate(pairs)]
    for get in gets:
        get.start()
    me = strip_ref[0]
    odd = me & 1
    has_far = (me > 0) & (me < strips - 1)
    near_row = pl.multiple_of((1 - odd) * 2 * strip, strip)
    far_row = pl.multiple_of(odd * 2 * strip, strip)
    tiles = width // LANES
    for p in range(2):
        for j in range(tiles):
            tile = pl.ds(j * LANES, LANES)
            ext[p, j, pl.ds(strip, strip), :] = pair_ref[1 - odd, p, :, tile].astype(jnp.float32)
            ext[p, j, pl.ds(near_row, strip), :] = near_ref[p, :, tile].astype(jnp.float32)
            far = pair_ref[odd, p, :, tile].astype(jnp.float32)
            ext[p, j, pl.ds(far_row, strip), :] = jnp.where(has_far, far, 0.0)
    placed[...] = jnp.zeros_like(placed)
    wave_a[...] = jnp.zeros_like(wave_a)
    for get in gets:
        get.wait()
    part = 16
    lane = lane_index((part, LANES))
    count = counts_ref[0, 0]
    slots = amp_ref.shape[0]
    spots = range(0, length, part)

    def place_of(f):
        col = columns_ref[0, f]
        return rows_ref[0, f], col // LANES, lax.rem(col, LANES)

    def cut(f, column):
        row, first, rest = place_of(f)
        back = lax.rem(LANES - rest, LANES)
        low = lane < LANES - rest
        for at in spots:
            window = []
            for p in range(2):
                turned = [pltpu.roll(ext[p, first + j, pl.ds(row + at, part), :], back, axis=1) for j in range(3)]
                window.append([jnp.where(low, turned[j], turned[j + 1]) for j in range(2)])
            for j in range(2):
                tile = pl.ds(j * LANES, LANES)
                pr = probe_ref[0, pl.ds(at, part), tile].astype(jnp.float32)
                pi = probe_ref[1, pl.ds(at, part), tile].astype(jnp.float32)
                xr, xi = window[0][j], window[1][j]
                column[pl.ds(at, part), tile] = (pr * xr - pi * xi).astype(jnp.bfloat16)
                column[pl.ds(length + at, part), tile] = (pr * xi + pi * xr).astype(jnp.bfloat16)

    def left(matrix, column, side):
        for m in range(0, 2 * length, MROWS):
            value = jnp.dot(matrix[pl.ds(m, MROWS), :], column[...], preferred_element_type=jnp.float32)
            p, r = divmod(m, length)
            if MROWS > length:
                side[:, pl.ds(0, length)] = value[:length].astype(jnp.bfloat16)
                side[:, pl.ds(length, length)] = value[length:].astype(jnp.bfloat16)
            else:
                side[pl.ds(r, MROWS), pl.ds(p * length, length)] = value.astype(jnp.bfloat16)

    def compare(f, side, column):
        for at in spots:
            if at % CHUNK == 0:
                far = jnp.dot(side[pl.ds(at, CHUNK), :], inv_ref[...], preferred_element_type=jnp.float32)
            rs = slice(at % CHUNK, at % CHUNK + part)
            fr = far[rs, :length]
            fi = far[rs, length:]
            factor = 1.0 - amp_ref[f, pl.ds(at, part), :].astype(jnp.float32) * lax.rsqrt(fr * fr + fi * fi + 1.0)
            column[pl.ds(at, part), :] = (fr * factor).astype(jnp.bfloat16)
            column[pl.ds(length + at, part), :] = (fi * factor).astype(jnp.bfloat16)

    def turn_back(f, side, wave):
        rest = place_of(f)[2]
        for at in spots:
            if at % CHUNK == 0:
                back = jnp.dot(side[pl.ds(at, CHUNK), :], fwd_ref[...], preferred_element_type=jnp.float32)
            rs = slice(at % CHUNK, at % CHUNK + part)
            for j in range(2):
                tile = pl.ds(j * LANES, LANES)
                pr = probe_ref[0, pl.ds(at, part), tile].astype(jnp.float32)
                pi = probe_ref[1, pl.ds(at, part), tile].astype(jnp.float32)
                br = back[rs, j * LANES : (j + 1) * LANES]
                bi = back[rs, length + j * LANES : length + (j + 1) * LANES]
                wave[0, j, pl.ds(at, part), :] = pltpu.roll(pr * br + pi * bi, rest, axis=1)
                wave[1, j, pl.ds(at, part), :] = pltpu.roll(pr * bi - pi * br, rest, axis=1)

    def add(f, wave):
        row, first, rest = place_of(f)
        high = lane >= rest
        for at in spots:
            for p in range(2):
                one = wave[p, 0, pl.ds(at, part), :]
                two = wave[p, 1, pl.ds(at, part), :]
                pieces = [jnp.where(high, one, 0.0), jnp.where(high, two, one), jnp.where(high, 0.0, two)]
                for j in range(3):
                    spot = (p, first + j, pl.ds(row + at, part), slice(None))
                    placed[spot] = placed[spot] + pieces[j]

    def one_frame(f, _):
        left(fwd_ref, column_a, side_a)
        cut(jnp.minimum(f + 1, slots - 1), column_a)
        add(jnp.maximum(f - 1, 0), wave_a)
        compare(f, side_a, column_b)
        left(inv_ref, column_b, side_b)
        turn_back(f, side_b, wave_a)
        return 0

    cut(0, column_a)
    lax.fori_loop(0, count, one_frame, 0)
    add(count - 1, wave_a)
    for p in range(2):
        for j in range(tiles):
            tile = pl.ds(j * LANES, LANES)
            mid_ref[p, :, tile] = placed[p, j, pl.ds(strip, strip), :]
            to_near_ref[p, :, tile] = placed[p, j, pl.ds(near_row, strip), :].astype(to_near_ref.dtype)
            far = jnp.where(has_far, placed[p, j, pl.ds(far_row, strip), :], 0.0)
            send_ref[odd, p, :, tile] = far.astype(send_ref.dtype)


def frames(me, strips, counts, rows, columns, pair, near, probe, amplitudes):
    length = probe.shape[1]
    parts, strip, width = near.shape
    fwd, inv = (jnp.asarray(m) for m in dft_blocks(length))
    smem = pl.BlockSpec(memory_space=SMEM)
    hbm = pl.BlockSpec(memory_space=pltpu.HBM)
    vmem = pl.BlockSpec(memory_space=VMEM)
    return pl.pallas_call(
        functools.partial(frames_body, strips),
        out_shape=(
            jax.ShapeDtypeStruct(near.shape, jnp.float32),
            jax.ShapeDtypeStruct(near.shape, jnp.bfloat16),
            jax.ShapeDtypeStruct(pair.shape, jnp.bfloat16),
        ),
        in_specs=[smem] * 2 + [hbm] * 2 + [vmem] * 2 + [hbm] + [vmem] * 3,
        out_specs=(vmem,) * 3,
        scratch_shapes=[
            pltpu.SemaphoreType.DMA((3,)),
            SMEM(rows.shape, rows.dtype),
            SMEM(columns.shape, columns.dtype),
            VMEM(probe.shape, probe.dtype),
            VMEM((parts, width // LANES + 1, 3 * strip, LANES), jnp.float32),
            VMEM((parts, width // LANES + 1, 3 * strip, LANES), jnp.float32),
            VMEM((2 * length, length), jnp.bfloat16),
            VMEM((2 * length, length), jnp.bfloat16),
            VMEM((length, 2 * length), jnp.bfloat16),
            VMEM((length, 2 * length), jnp.bfloat16),
            VMEM((2, length // LANES, length, LANES), jnp.float32),
        ],
        compiler_params=pltpu.CompilerParams(vmem_limit_bytes=32 << 20),
        name="frames",
    )(me, counts, in_hbm(rows), in_hbm(columns), pair, near, in_hbm(probe), fwd, inv, amplitudes)


def per_device(slab, taps, offsets, probe, scan_rows, scan_columns, counts, amplitudes):
    parts, rows, width = slab.shape[1:]
    angles = lax.axis_size("ang")
    strips = lax.axis_size("strip")
    block = parts * rows // angles
    me = lax.axis_index("strip")
    own_half = (me.astype(jnp.uint32) & 1) ^ 1
    place, half = me.astype(jnp.int32).reshape(1), own_half.astype(jnp.int32).reshape(1)
    groups = [
        [a * strips + s % strips for s in (first, first + 1) for a in range(angles)] for first in range(1, strips, 2)
    ]

    def swap(x):
        return lax.ppermute(x, "strip", [(s, s ^ 1) for s in range(strips)])

    def exchange(x):
        return lax.all_to_all(x, "ang", 0, 0, tiled=True)

    def pair_exchange(x):
        return lax.all_to_all(x, ("ang", "strip"), 0, 0, axis_index_groups=groups, tiled=True)

    mixed = exchange(slab.reshape(angles, block, width))
    pair = pair_exchange(shear(mixed, taps, offsets, 1, 2, place, half)).reshape(2, parts, rows, width)
    near = swap(lax.dynamic_index_in_dim(pair, own_half, 0, keepdims=False))
    mid, to_near, send = frames(place, strips, counts, scan_rows, scan_columns, pair, near, probe, amplitudes[0])
    own = (mid + swap(to_near).astype(jnp.float32)).astype(jnp.bfloat16)
    send = lax.dynamic_update_index_in_dim(send, own, own_half, 0)
    mixed = pair_exchange(send.reshape(2 * angles, block, width))
    result = exchange(shear(mixed, taps, offsets, -1, 1))
    return result.reshape(1, parts, rows, width).astype(jnp.float32)


def solution(mesh):
    return jax.shard_map(
        per_device,
        mesh=mesh,
        in_specs=(
            P("ang", None, "strip", None),
            P(),
            P(),
            P(),
            P("ang", "strip"),
            P("ang", "strip"),
            P("ang", "strip"),
            P("ang", "strip", None, None),
        ),
        out_specs=P("ang", None, "strip", None),
        check_vma=False,
    )
```

```python
import functools
import math

import jax
import jax.numpy as jnp
import numpy as np
from jax import lax
from jax.experimental import pallas as pl
from jax.experimental.pallas import tpu as pltpu
from jax.sharding import PartitionSpec as P

MAXSHIFT = 64
LANES = 128
MROWS = 256
CHUNK = 256
VMEM = pltpu.VMEM
SMEM = pltpu.SMEM


def dft_blocks(length):
    index = np.arange(length, dtype=np.int64)
    product = index[:, None] * index[None, :] % length
    phase = product.astype(np.float32) * np.float32(2.0 * math.pi / length)
    scale = np.float32(1.0 / math.sqrt(length))
    cosine = (np.cos(phase) * scale).astype(jnp.bfloat16)
    sine = (np.sin(phase) * scale).astype(jnp.bfloat16)
    forward = np.block([[cosine, sine], [-sine, cosine]])
    inverse = np.block([[cosine, -sine], [sine, cosine]])
    return forward, inverse


def in_hbm(x):
    return pltpu.with_memory_space_constraint(x, pltpu.HBM)


def lane_index(shape):
    return lax.broadcasted_iota(jnp.int32, shape, len(shape) - 1)


def shear_body(sign, ahead, taps_hbm, offsets_hbm, x_ref, *refs):
    o_ref, taps_ref, offsets_ref, ready, copies = refs[ahead:]
    count = taps_ref.shape[1]
    rows, width = x_ref.shape[1:]
    tiles = width // LANES + 1
    ntaps = taps_ref.shape[0]
    left = MAXSHIFT if sign > 0 else MAXSHIFT + ntaps - 1
    get_taps = pltpu.make_async_copy(taps_hbm, taps_ref, ready.at[0])
    get_offsets = pltpu.make_async_copy(offsets_hbm, offsets_ref, ready.at[1])
    get_taps.start()
    get_offsets.start()

    def lay_out(s, _):
        value = x_ref[s].astype(jnp.float32)
        for again in range(1, x_ref.shape[0] // count):
            value = value + x_ref[s + again * count].astype(jnp.float32)
        value = value.astype(jnp.bfloat16).astype(jnp.float32)
        value = jnp.concatenate([value, jnp.zeros((rows, LANES), jnp.float32)], axis=1)
        for k in range(ntaps):
            moved = pltpu.roll(value, left - k, axis=1)
            for j in range(tiles):
                copies[s, k, j] = moved[:, j * LANES : (j + 1) * LANES]
        return 0

    lax.fori_loop(0, count, lay_out, 0, unroll=4)
    get_taps.wait()
    get_offsets.wait()
    lane = lane_index((rows, LANES))

    def one(d, _):
        total = [jnp.zeros((rows, LANES), jnp.float32) for _ in range(tiles - 1)]
        for s in range(count):
            angle, depth = (d, s) if sign > 0 else (s, d)
            amount = MAXSHIFT + sign * offsets_ref[angle, depth]
            back = lax.rem(LANES - amount, LANES)
            keep = lane < LANES - amount
            weights = [taps_ref[k if sign > 0 else ntaps - 1 - k, angle, depth] for k in range(ntaps)]
            turned = []
            for j in range(tiles):
                terms = [weights[k] * copies[s, k, j] for k in range(ntaps)]
                both = (terms[0] + terms[1]) + (terms[2] + terms[3])
                turned.append(pltpu.roll(both, back, axis=1))
            for j in range(tiles - 1):
                total[j] = total[j] + jnp.where(keep, turned[j], turned[j + 1])
        for j in range(tiles - 1):
            out = total[j].astype(o_ref.dtype)
            for again in range(o_ref.shape[0] // count):
                o_ref[d + again * count, :, pl.ds(j * LANES, LANES)] = out
        return 0

    lax.fori_loop(0, count, one, 0, unroll=4)


def shear(x, taps, offsets, sign, copies, *ahead):
    rows, width = x.shape[1:]
    count = taps.shape[1]
    tiles = width // LANES + 1
    return pl.pallas_call(
        functools.partial(shear_body, sign, len(ahead)),
        out_shape=jax.ShapeDtypeStruct((copies * count, rows, width), jnp.bfloat16),
        in_specs=[
            pl.BlockSpec(memory_space=pltpu.HBM),
            pl.BlockSpec(memory_space=pltpu.HBM),
            pl.BlockSpec(memory_space=VMEM),
        ]
        + [pl.BlockSpec(memory_space=SMEM)] * len(ahead),
        out_specs=pl.BlockSpec(memory_space=VMEM),
        scratch_shapes=[
            SMEM(taps.shape, taps.dtype),
            SMEM(offsets.shape, offsets.dtype),
            pltpu.SemaphoreType.DMA((2,)),
            VMEM((count, taps.shape[0], tiles, rows, LANES), jnp.float32),
        ],
        compiler_params=pltpu.CompilerParams(vmem_limit_bytes=16 << 20),
        name="shear_forward" if sign > 0 else "shear_back",
    )(in_hbm(taps), in_hbm(offsets), x, *ahead)


def frames_body(
    strips, strip_ref, counts_ref, rows_hbm, columns_hbm, pair_ref, near_ref, probe_hbm, fwd_ref, inv_ref, amp_ref,
    mid_ref, to_near_ref, send_ref,
    ready, rows_ref, columns_ref, probe_ref, ext, placed,
    column_a, column_b, side_a, side_b, wave_a,
):
    length = probe_ref.shape[1]
    strip, width = near_ref.shape[1:]
    pairs = [
        (rows_hbm, rows_ref),
        (columns_hbm, columns_ref),
        (probe_hbm, probe_ref),
    ]
    gets = [pltpu.make_async_copy(src, dst, ready.at[i]) for i, (src, dst) in enumerate(pairs)]
    for get in gets:
        get.start()
    me = strip_ref[0]
    odd = me & 1
    has_far = (me > 0) & (me < strips - 1)
    near_row = pl.multiple_of((1 - odd) * 2 * strip, strip)
    far_row = pl.multiple_of(odd * 2 * strip, strip)
    tiles = width // LANES
    for p in range(2):
        for j in range(tiles):
            tile = pl.ds(j * LANES, LANES)
            ext[p, j, pl.ds(strip, strip), :] = pair_ref[1 - odd, p, :, tile].astype(jnp.float32)
            ext[p, j, pl.ds(near_row, strip), :] = near_ref[p, :, tile].astype(jnp.float32)
            far = pair_ref[odd, p, :, tile].astype(jnp.float32)
            ext[p, j, pl.ds(far_row, strip), :] = jnp.where(has_far, far, 0.0)
    placed[...] = jnp.zeros_like(placed)
    wave_a[...] = jnp.zeros_like(wave_a)
    for get in gets:
        get.wait()
    part = 16
    lane = lane_index((part, LANES))
    count = counts_ref[0, 0]
    slots = amp_ref.shape[0]
    spots = range(0, length, part)

    def place_of(f):
        col = columns_ref[0, f]
        return rows_ref[0, f], col // LANES, lax.rem(col, LANES)

    def cut(f, column):
        row, first, rest = place_of(f)
        back = lax.rem(LANES - rest, LANES)
        low = lane < LANES - rest
        for at in spots:
            window = []
            for p in range(2):
                turned = [pltpu.roll(ext[p, first + j, pl.ds(row + at, part), :].astype(jnp.bfloat16), back, axis=1).astype(jnp.float32) for j in range(3)]
                window.append([jnp.where(low, turned[j], turned[j + 1]) for j in range(2)])
            for j in range(2):
                tile = pl.ds(j * LANES, LANES)
                pr = probe_ref[0, pl.ds(at, part), tile].astype(jnp.float32)
                pi = probe_ref[1, pl.ds(at, part), tile].astype(jnp.float32)
                xr, xi = window[0][j], window[1][j]
                column[pl.ds(at, part), tile] = (pr * xr - pi * xi).astype(jnp.bfloat16)
                column[pl.ds(length + at, part), tile] = (pr * xi + pi * xr).astype(jnp.bfloat16)

    def left(matrix, column, side):
        for m in range(0, 2 * length, MROWS):
            value = jnp.dot(matrix[pl.ds(m, MROWS), :], column[...], preferred_element_type=jnp.float32)
            p, r = divmod(m, length)
            if MROWS > length:
                side[:, pl.ds(0, length)] = value[:length].astype(jnp.bfloat16)
                side[:, pl.ds(length, length)] = value[length:].astype(jnp.bfloat16)
            else:
                side[pl.ds(r, MROWS), pl.ds(p * length, length)] = value.astype(jnp.bfloat16)

    def compare(f, side, column):
        for at in spots:
            if at % CHUNK == 0:
                far = jnp.dot(side[pl.ds(at, CHUNK), :], inv_ref[...], preferred_element_type=jnp.float32)
            rs = slice(at % CHUNK, at % CHUNK + part)
            fr = far[rs, :length]
            fi = far[rs, length:]
            factor = 1.0 - amp_ref[f, pl.ds(at, part), :].astype(jnp.float32) * lax.rsqrt(fr * fr + fi * fi + 1.0)
            column[pl.ds(at, part), :] = (fr * factor).astype(jnp.bfloat16)
            column[pl.ds(length + at, part), :] = (fi * factor).astype(jnp.bfloat16)

    def turn_back(f, side, wave):
        rest = place_of(f)[2]
        for at in spots:
            if at % CHUNK == 0:
                back = jnp.dot(side[pl.ds(at, CHUNK), :], fwd_ref[...], preferred_element_type=jnp.float32)
            rs = slice(at % CHUNK, at % CHUNK + part)
            for j in range(2):
                tile = pl.ds(j * LANES, LANES)
                pr = probe_ref[0, pl.ds(at, part), tile].astype(jnp.float32)
                pi = probe_ref[1, pl.ds(at, part), tile].astype(jnp.float32)
                br = back[rs, j * LANES : (j + 1) * LANES]
                bi = back[rs, length + j * LANES : length + (j + 1) * LANES]
                wave[0, j, pl.ds(at, part), :] = pltpu.roll(pr * br + pi * bi, rest, axis=1)
                wave[1, j, pl.ds(at, part), :] = pltpu.roll(pr * bi - pi * br, rest, axis=1)

    def add(f, wave):
        row, first, rest = place_of(f)
        high = lane >= rest
        for at in spots:
            for p in range(2):
                one = wave[p, 0, pl.ds(at, part), :]
                two = wave[p, 1, pl.ds(at, part), :]
                pieces = [jnp.where(high, one, 0.0), jnp.where(high, two, one), jnp.where(high, 0.0, two)]
                for j in range(3):
                    spot = (p, first + j, pl.ds(row + at, part), slice(None))
                    placed[spot] = placed[spot] + pieces[j]

    def one_frame(f, _):
        left(fwd_ref, column_a, side_a)
        cut(jnp.minimum(f + 1, slots - 1), column_a)
        add(jnp.maximum(f - 1, 0), wave_a)
        compare(f, side_a, column_b)
        left(inv_ref, column_b, side_b)
        turn_back(f, side_b, wave_a)
        return 0

    cut(0, column_a)
    lax.fori_loop(0, count, one_frame, 0)
    add(count - 1, wave_a)
    for p in range(2):
        for j in range(tiles):
            tile = pl.ds(j * LANES, LANES)
            mid_ref[p, :, tile] = placed[p, j, pl.ds(strip, strip), :]
            to_near_ref[p, :, tile] = placed[p, j, pl.ds(near_row, strip), :].astype(to_near_ref.dtype)
            far = jnp.where(has_far, placed[p, j, pl.ds(far_row, strip), :], 0.0)
            send_ref[odd, p, :, tile] = far.astype(send_ref.dtype)


def frames(me, strips, counts, rows, columns, pair, near, probe, amplitudes):
    length = probe.shape[1]
    parts, strip, width = near.shape
    fwd, inv = (jnp.asarray(m) for m in dft_blocks(length))
    smem = pl.BlockSpec(memory_space=SMEM)
    hbm = pl.BlockSpec(memory_space=pltpu.HBM)
    vmem = pl.BlockSpec(memory_space=VMEM)
    return pl.pallas_call(
        functools.partial(frames_body, strips),
        out_shape=(
            jax.ShapeDtypeStruct(near.shape, jnp.float32),
            jax.ShapeDtypeStruct(near.shape, jnp.bfloat16),
            jax.ShapeDtypeStruct(pair.shape, jnp.bfloat16),
        ),
        in_specs=[smem] * 2 + [hbm] * 2 + [vmem] * 2 + [hbm] + [vmem] * 3,
        out_specs=(vmem,) * 3,
        scratch_shapes=[
            pltpu.SemaphoreType.DMA((3,)),
            SMEM(rows.shape, rows.dtype),
            SMEM(columns.shape, columns.dtype),
            VMEM(probe.shape, probe.dtype),
            VMEM((parts, width // LANES + 1, 3 * strip, LANES), jnp.float32),
            VMEM((parts, width // LANES + 1, 3 * strip, LANES), jnp.float32),
            VMEM((2 * length, length), jnp.bfloat16),
            VMEM((2 * length, length), jnp.bfloat16),
            VMEM((length, 2 * length), jnp.bfloat16),
            VMEM((length, 2 * length), jnp.bfloat16),
            VMEM((2, length // LANES, length, LANES), jnp.float32),
        ],
        compiler_params=pltpu.CompilerParams(vmem_limit_bytes=32 << 20),
        name="frames",
    )(me, counts, in_hbm(rows), in_hbm(columns), pair, near, in_hbm(probe), fwd, inv, amplitudes)


def per_device(slab, taps, offsets, probe, scan_rows, scan_columns, counts, amplitudes):
    parts, rows, width = slab.shape[1:]
    angles = lax.axis_size("ang")
    strips = lax.axis_size("strip")
    block = parts * rows // angles
    me = lax.axis_index("strip")
    own_half = (me.astype(jnp.uint32) & 1) ^ 1
    place, half = me.astype(jnp.int32).reshape(1), own_half.astype(jnp.int32).reshape(1)
    groups = [
        [a * strips + s % strips for s in (first, first + 1) for a in range(angles)] for first in range(1, strips, 2)
    ]

    def swap(x):
        return lax.ppermute(x, "strip", [(s, s ^ 1) for s in range(strips)])

    def exchange(x):
        return lax.all_to_all(x, "ang", 0, 0, tiled=True)

    def pair_exchange(x):
        return lax.all_to_all(x, ("ang", "strip"), 0, 0, axis_index_groups=groups, tiled=True)

    mixed = exchange(slab.reshape(angles, block, width))
    pair = pair_exchange(shear(mixed, taps, offsets, 1, 2, place, half)).reshape(2, parts, rows, width)
    near = swap(lax.dynamic_index_in_dim(pair, own_half, 0, keepdims=False))
    mid, to_near, send = frames(place, strips, counts, scan_rows, scan_columns, pair, near, probe, amplitudes[0])
    own = (mid + swap(to_near).astype(jnp.float32)).astype(jnp.bfloat16)
    send = lax.dynamic_update_index_in_dim(send, own, own_half, 0)
    mixed = pair_exchange(send.reshape(2 * angles, block, width))
    result = exchange(shear(mixed, taps, offsets, -1, 1))
    return result.reshape(1, parts, rows, width).astype(jnp.float32)


def solution(mesh):
    return jax.shard_map(
        per_device,
        mesh=mesh,
        in_specs=(
            P("ang", None, "strip", None),
            P(),
            P(),
            P(),
            P("ang", "strip"),
            P("ang", "strip"),
            P("ang", "strip"),
            P("ang", "strip", None, None),
        ),
        out_specs=P("ang", None, "strip", None),
        check_vma=False,
    )
```

```python
import functools
import math

import jax
import jax.numpy as jnp
import numpy as np
from jax import lax
from jax.experimental import pallas as pl
from jax.experimental.pallas import tpu as pltpu
from jax.sharding import PartitionSpec as P

MAXSHIFT = 64
LANES = 128
MROWS = 256
CHUNK = 256
VMEM = pltpu.VMEM
SMEM = pltpu.SMEM


def dft_blocks(length):
    index = np.arange(length, dtype=np.int64)
    product = index[:, None] * index[None, :] % length
    phase = product.astype(np.float32) * np.float32(2.0 * math.pi / length)
    scale = np.float32(1.0 / math.sqrt(length))
    cosine = (np.cos(phase) * scale).astype(jnp.bfloat16)
    sine = (np.sin(phase) * scale).astype(jnp.bfloat16)
    forward = np.block([[cosine, sine], [-sine, cosine]])
    inverse = np.block([[cosine, -sine], [sine, cosine]])
    return forward, inverse


def in_hbm(x):
    return pltpu.with_memory_space_constraint(x, pltpu.HBM)


def lane_index(shape):
    return lax.broadcasted_iota(jnp.int32, shape, len(shape) - 1)


def shear_body(sign, ahead, taps_hbm, offsets_hbm, x_ref, *refs):
    o_ref, taps_ref, offsets_ref, ready, copies = refs[ahead:]
    count = taps_ref.shape[1]
    rows, width = x_ref.shape[1:]
    tiles = width // LANES + 1
    ntaps = taps_ref.shape[0]
    left = MAXSHIFT if sign > 0 else MAXSHIFT + ntaps - 1
    get_taps = pltpu.make_async_copy(taps_hbm, taps_ref, ready.at[0])
    get_offsets = pltpu.make_async_copy(offsets_hbm, offsets_ref, ready.at[1])
    get_taps.start()
    get_offsets.start()

    def lay_out(s, _):
        value = x_ref[s].astype(jnp.float32)
        for again in range(1, x_ref.shape[0] // count):
            value = value + x_ref[s + again * count].astype(jnp.float32)
        value = value.astype(jnp.bfloat16).astype(jnp.float32)
        value = jnp.concatenate([value, jnp.zeros((rows, LANES), jnp.float32)], axis=1)
        for k in range(ntaps):
            moved = pltpu.roll(value, left - k, axis=1)
            for j in range(tiles):
                copies[s, k, j] = moved[:, j * LANES : (j + 1) * LANES]
        return 0

    lax.fori_loop(0, count, lay_out, 0, unroll=4)
    get_taps.wait()
    get_offsets.wait()
    lane = lane_index((rows, LANES))

    def one(d, _):
        total = [jnp.zeros((rows, LANES), jnp.float32) for _ in range(tiles - 1)]
        for s in range(count):
            angle, depth = (d, s) if sign > 0 else (s, d)
            amount = MAXSHIFT + sign * offsets_ref[angle, depth]
            back = lax.rem(LANES - amount, LANES)
            keep = lane < LANES - amount
            weights = [taps_ref[k if sign > 0 else ntaps - 1 - k, angle, depth] for k in range(ntaps)]
            turned = []
            for j in range(tiles):
                terms = [weights[k] * copies[s, k, j] for k in range(ntaps)]
                both = (terms[0] + terms[1]) + (terms[2] + terms[3])
                turned.append(pltpu.roll(both, back, axis=1))
            for j in range(tiles - 1):
                total[j] = total[j] + jnp.where(keep, turned[j], turned[j + 1])
        for j in range(tiles - 1):
            out = total[j].astype(o_ref.dtype)
            for again in range(o_ref.shape[0] // count):
                o_ref[d + again * count, :, pl.ds(j * LANES, LANES)] = out
        return 0

    lax.fori_loop(0, count, one, 0, unroll=4)


def shear(x, taps, offsets, sign, copies, *ahead):
    rows, width = x.shape[1:]
    count = taps.shape[1]
    tiles = width // LANES + 1
    return pl.pallas_call(
        functools.partial(shear_body, sign, len(ahead)),
        out_shape=jax.ShapeDtypeStruct((copies * count, rows, width), jnp.bfloat16),
        in_specs=[
            pl.BlockSpec(memory_space=pltpu.HBM),
            pl.BlockSpec(memory_space=pltpu.HBM),
            pl.BlockSpec(memory_space=VMEM),
        ]
        + [pl.BlockSpec(memory_space=SMEM if x.dtype == jnp.int32 else VMEM) for x in ahead],
        out_specs=pl.BlockSpec(memory_space=VMEM),
        scratch_shapes=[
            SMEM(taps.shape, taps.dtype),
            SMEM(offsets.shape, offsets.dtype),
            pltpu.SemaphoreType.DMA((2,)),
            VMEM((count, taps.shape[0], tiles, rows, LANES), jnp.float32),
        ],
        compiler_params=pltpu.CompilerParams(vmem_limit_bytes=16 << 20),
        name="shear_forward" if sign > 0 else "shear_back",
    )(in_hbm(taps), in_hbm(offsets), x, *ahead)


def frames_body(
    strips, strip_ref, counts_ref, rows_ref, columns_ref, pair_ref, near_ref, probe_ref, fwd_ref, inv_ref, amp_ref,
    mid_ref, to_near_ref, send_ref,
    ext, placed,
    column_a, column_b, side_a, side_b, wave_a,
):
    length = probe_ref.shape[1]
    strip, width = near_ref.shape[1:]
    me = strip_ref[0]
    odd = me & 1
    has_far = (me > 0) & (me < strips - 1)
    near_row = pl.multiple_of((1 - odd) * 2 * strip, strip)
    far_row = pl.multiple_of(odd * 2 * strip, strip)
    tiles = width // LANES
    for p in range(2):
        for j in range(tiles):
            tile = pl.ds(j * LANES, LANES)
            ext[p, j, pl.ds(strip, strip), :] = pair_ref[1 - odd, p, :, tile].astype(jnp.float32)
            ext[p, j, pl.ds(near_row, strip), :] = near_ref[p, :, tile].astype(jnp.float32)
            far = pair_ref[odd, p, :, tile].astype(jnp.float32)
            ext[p, j, pl.ds(far_row, strip), :] = jnp.where(has_far, far, 0.0)
    placed[...] = jnp.zeros_like(placed)
    wave_a[...] = jnp.zeros_like(wave_a)
    part = 16
    lane = lane_index((part, LANES))
    count = counts_ref[0, 0]
    slots = amp_ref.shape[0]
    spots = range(0, length, part)

    def place_of(f):
        col = columns_ref[0, f]
        return rows_ref[0, f], col // LANES, lax.rem(col, LANES)

    def cut(f, column):
        row, first, rest = place_of(f)
        back = lax.rem(LANES - rest, LANES)
        low = lane < LANES - rest
        for at in spots:
            window = []
            for p in range(2):
                turned = [pltpu.roll(ext[p, first + j, pl.ds(row + at, part), :].astype(jnp.bfloat16), back, axis=1).astype(jnp.float32) for j in range(3)]
                window.append([jnp.where(low, turned[j], turned[j + 1]) for j in range(2)])
            for j in range(2):
                tile = pl.ds(j * LANES, LANES)
                pr = probe_ref[0, pl.ds(at, part), tile].astype(jnp.float32)
                pi = probe_ref[1, pl.ds(at, part), tile].astype(jnp.float32)
                xr, xi = window[0][j], window[1][j]
                column[pl.ds(at, part), tile] = (pr * xr - pi * xi).astype(jnp.bfloat16)
                column[pl.ds(length + at, part), tile] = (pr * xi + pi * xr).astype(jnp.bfloat16)

    def left(matrix, column, side):
        for m in range(0, 2 * length, MROWS):
            value = jnp.dot(matrix[pl.ds(m, MROWS), :], column[...], preferred_element_type=jnp.float32)
            p, r = divmod(m, length)
            if MROWS > length:
                side[:, pl.ds(0, length)] = value[:length].astype(jnp.bfloat16)
                side[:, pl.ds(length, length)] = value[length:].astype(jnp.bfloat16)
            else:
                side[pl.ds(r, MROWS), pl.ds(p * length, length)] = value.astype(jnp.bfloat16)

    def compare(f, side, column):
        for at in spots:
            if at % CHUNK == 0:
                far = jnp.dot(side[pl.ds(at, CHUNK), :], inv_ref[...], preferred_element_type=jnp.float32)
            rs = slice(at % CHUNK, at % CHUNK + part)
            fr = far[rs, :length]
            fi = far[rs, length:]
            factor = 1.0 - amp_ref[f, pl.ds(at, part), :].astype(jnp.float32) * lax.rsqrt(fr * fr + fi * fi + 1.0)
            column[pl.ds(at, part), :] = (fr * factor).astype(jnp.bfloat16)
            column[pl.ds(length + at, part), :] = (fi * factor).astype(jnp.bfloat16)

    def turn_back(f, side, wave):
        rest = place_of(f)[2]
        for at in spots:
            if at % CHUNK == 0:
                back = jnp.dot(side[pl.ds(at, CHUNK), :], fwd_ref[...], preferred_element_type=jnp.float32)
            rs = slice(at % CHUNK, at % CHUNK + part)
            for j in range(2):
                tile = pl.ds(j * LANES, LANES)
                pr = probe_ref[0, pl.ds(at, part), tile].astype(jnp.float32)
                pi = probe_ref[1, pl.ds(at, part), tile].astype(jnp.float32)
                br = back[rs, j * LANES : (j + 1) * LANES]
                bi = back[rs, length + j * LANES : length + (j + 1) * LANES]
                wave[0, j, pl.ds(at, part), :] = pltpu.roll(pr * br + pi * bi, rest, axis=1)
                wave[1, j, pl.ds(at, part), :] = pltpu.roll(pr * bi - pi * br, rest, axis=1)

    def add(f, wave):
        row, first, rest = place_of(f)
        high = lane >= rest
        for at in spots:
            for p in range(2):
                one = wave[p, 0, pl.ds(at, part), :]
                two = wave[p, 1, pl.ds(at, part), :]
                pieces = [jnp.where(high, one, 0.0), jnp.where(high, two, one), jnp.where(high, 0.0, two)]
                for j in range(3):
                    spot = (p, first + j, pl.ds(row + at, part), slice(None))
                    placed[spot] = placed[spot] + pieces[j]

    def one_frame(f, _):
        left(fwd_ref, column_a, side_a)
        cut(jnp.minimum(f + 1, slots - 1), column_a)
        add(jnp.maximum(f - 1, 0), wave_a)
        compare(f, side_a, column_b)
        left(inv_ref, column_b, side_b)
        turn_back(f, side_b, wave_a)
        return 0

    cut(0, column_a)
    lax.fori_loop(0, count, one_frame, 0)
    add(count - 1, wave_a)
    for p in range(2):
        for j in range(tiles):
            tile = pl.ds(j * LANES, LANES)
            mid_ref[p, :, tile] = placed[p, j, pl.ds(strip, strip), :]
            to_near_ref[p, :, tile] = placed[p, j, pl.ds(near_row, strip), :].astype(to_near_ref.dtype)
            far = jnp.where(has_far, placed[p, j, pl.ds(far_row, strip), :], 0.0)
            send_ref[odd, p, :, tile] = far.astype(send_ref.dtype)


def frames(me, strips, counts, rows, columns, pair, near, probe, amplitudes):
    length = probe.shape[1]
    parts, strip, width = near.shape
    fwd, inv = (jnp.asarray(m) for m in dft_blocks(length))
    smem = pl.BlockSpec(memory_space=SMEM)
    vmem = pl.BlockSpec(memory_space=VMEM)
    return pl.pallas_call(
        functools.partial(frames_body, strips),
        out_shape=(
            jax.ShapeDtypeStruct(near.shape, jnp.float32),
            jax.ShapeDtypeStruct(near.shape, jnp.bfloat16),
            jax.ShapeDtypeStruct(pair.shape, jnp.bfloat16),
        ),
        in_specs=[smem] * 4 + [vmem] * 6,
        out_specs=(vmem,) * 3,
        scratch_shapes=[
            VMEM((parts, width // LANES + 1, 3 * strip, LANES), jnp.float32),
            VMEM((parts, width // LANES + 1, 3 * strip, LANES), jnp.float32),
            VMEM((2 * length, length), jnp.bfloat16),
            VMEM((2 * length, length), jnp.bfloat16),
            VMEM((length, 2 * length), jnp.bfloat16),
            VMEM((length, 2 * length), jnp.bfloat16),
            VMEM((2, length // LANES, length, LANES), jnp.float32),
        ],
        compiler_params=pltpu.CompilerParams(vmem_limit_bytes=32 << 20),
        name="frames",
    )(me, counts, rows, columns, pair, near, probe, fwd, inv, amplitudes)


def per_device(slab, taps, offsets, probe, scan_rows, scan_columns, counts, amplitudes):
    parts, rows, width = slab.shape[1:]
    angles = lax.axis_size("ang")
    strips = lax.axis_size("strip")
    block = parts * rows // angles
    me = lax.axis_index("strip")
    own_half = (me.astype(jnp.uint32) & 1) ^ 1
    place, half = me.astype(jnp.int32).reshape(1), own_half.astype(jnp.int32).reshape(1)
    groups = [
        [a * strips + s % strips for s in (first, first + 1) for a in range(angles)] for first in range(1, strips, 2)
    ]

    def swap(x):
        return lax.ppermute(x, "strip", [(s, s ^ 1) for s in range(strips)])

    def exchange(x):
        return lax.all_to_all(x, "ang", 0, 0, tiled=True)

    def pair_exchange(x):
        return lax.all_to_all(x, ("ang", "strip"), 0, 0, axis_index_groups=groups, tiled=True)

    mixed = exchange(slab.reshape(angles, block, width))
    pair = pair_exchange(shear(mixed, taps, offsets, 1, 2, place, half, probe)).reshape(2, parts, rows, width)
    near = swap(lax.dynamic_index_in_dim(pair, own_half, 0, keepdims=False))
    mid, to_near, send = frames(place, strips, counts, scan_rows, scan_columns, pair, near, probe, amplitudes[0])
    own = (mid + swap(to_near).astype(jnp.float32)).astype(jnp.bfloat16)
    send = lax.dynamic_update_index_in_dim(send, own, own_half, 0)
    mixed = pair_exchange(send.reshape(2 * angles, block, width))
    result = exchange(shear(mixed, taps, offsets, -1, 1))
    return result.reshape(1, parts, rows, width).astype(jnp.float32)


def solution(mesh):
    return jax.shard_map(
        per_device,
        mesh=mesh,
        in_specs=(
            P("ang", None, "strip", None),
            P(),
            P(),
            P(),
            P("ang", "strip"),
            P("ang", "strip"),
            P("ang", "strip"),
            P("ang", "strip", None, None),
        ),
        out_specs=P("ang", None, "strip", None),
        check_vma=False,
    )
```
